32 devices in a mesh: gx: 2 (over y), gy: 4 (over x, core), gz: 4 (over z).
Axes of the slice: x: 2, y: 2, z: 4, core: 2. Of those that a mesh axis runs over, the one named last changes fastest.
Arguments:
- midpoints: float32 [3, 2, 4, 4, 1024], P(None, 'gx', 'gy', 'gz'), may hold values from 0 to 1
- line_vectors: float32 [3, 2, 4, 4, 1024], P(None, 'gx', 'gy', 'gz'), may hold values from -0.085 to 0.085
- burgers: float32 [3, 2, 4, 4, 1024], P(None, 'gx', 'gy', 'gz'), may hold values from -1.7 to 1.7
- live_mask: int32 [2, 4, 4, 1024], P('gx', 'gy', 'gz'), may hold values from 0 to 1, as said below
- pair_list: int32 [13, 2, 4, 4], P(None, 'gx', 'gy', 'gz'), may hold values 0 or 1
Outputs:
- forces: float32 [3, 2, 4, 4, 1024], P(None, 'gx', 'gy', 'gz')
The draws below stay inside these ranges and needn't reach their ends.
Inputs may be any that keep to these rules, and one draw needn't show every extreme that they name: `live_mask`: the live slots of each cell are a prefix of its 1024 slots; every cell has at least 256 live slots, and some cell has all 1024 live.
All inputs are finite; a program needn't handle non-finite values. No bound on the sum of `pair_list` on one device may be relied on, other than what follows from the above.
Results may differ from the reference program's by a relative error of at most 0.0003.
Values sent between devices are 32-bit elements; how exact they have to be, the bound alone decides.
A program may use at most 64 MiB of HBM per device.

```python
import jax
import jax.numpy as jnp
from jax import lax

SEG = 1024
NX = 2
NY = 4
NZ = 4


def draw_line_vectors(key, part):
    base = jax.random.uniform(jax.random.fold_in(key, 11), (3, NX, NY, NZ, SEG), jnp.float32, -1.0, 1.0)
    common = jax.random.uniform(jax.random.fold_in(key, 12), (3, NX, NY, NZ, 1), jnp.float32, -0.7, 0.7)
    return 0.05 * (base + common)


def draw_burgers(key, part):
    base = jax.random.uniform(jax.random.fold_in(key, 21), (3, NX, NY, NZ, SEG), jnp.float32, -1.0, 1.0)
    common = jax.random.uniform(jax.random.fold_in(key, 22), (3, NX, NY, NZ, 1), jnp.float32, -0.7, 0.7)
    return base + common


def draw_live_mask(key, part):
    counts = jax.random.randint(jax.random.fold_in(key, 31), (NX, NY, NZ), SEG // 4, SEG + 1)
    chosen = jax.random.randint(jax.random.fold_in(key, 32), (), 0, NX * NY * NZ)
    cell_ids = jnp.arange(NX * NY * NZ, dtype=jnp.int32).reshape(NX, NY, NZ)
    counts = jnp.where(cell_ids == chosen, SEG, counts)
    slots = jnp.arange(SEG, dtype=jnp.int32)
    return (slots[None, None, None, :] < counts[..., None]).astype(jnp.int32)


def with_ends(entries, own_key, smallest, top_value):
    spot = [jax.random.randint(jax.random.fold_in(own_key, axis), (), 0, length) for axis, length in enumerate(entries.shape)]
    longest = entries.shape.index(max(entries.shape))
    next_to = spot[:longest] + [(spot[longest] + 1) % entries.shape[longest]] + spot[longest + 1:]
    return entries.at[tuple(spot)].set(smallest).at[tuple(next_to)].set(top_value)


def block_scale(rng, dims, pieces, smallest, high):
    factor_of, own = 1.0, jax.random.fold_in(rng, 6)
    for axis_at, parts in pieces:
        steps = jnp.exp(jax.random.uniform(jax.random.fold_in(own, axis_at), (parts,), jnp.float32, smallest / len(pieces), high / len(pieces)))
        factor_of = factor_of * jnp.repeat(steps, dims[axis_at] // parts).reshape([-1 if axis == axis_at else 1 for axis in range(len(dims))])
    return factor_of


def setup_inputs(seed: int = 0) -> dict:
    seeds = jax.random.split(jax.random.key(seed), 6)
    midpoints = jnp.clip(1.0 * jax.random.uniform(seeds[0], (3, NX, NY, NZ, SEG), jnp.float32) ** block_scale(seeds[0], (3, NX, NY, NZ, SEG), ((1, 2), (2, 4), (3, 4)), -0.2, 0.2), 0.0, 1.0)
    line_vectors = draw_line_vectors(jax.random.fold_in(seeds[5], 71), 0)
    burgers = draw_burgers(jax.random.fold_in(seeds[5], 71), 0)
    live_mask = draw_live_mask(jax.random.fold_in(seeds[5], 71), 0)
    pair_list = with_ends((jax.random.randint(seeds[4], (13, NX, NY, NZ), 0, 2) < 1).astype(jnp.int32), jax.random.fold_in(seeds[4], 1), 0, 1)
    return {"midpoints": midpoints, "line_vectors": line_vectors, "burgers": burgers, "live_mask": live_mask, "pair_list": pair_list}


CORE_WIDTH = 0.1
SPLIT_WIDTH = 2.0
HIGHEST = lax.Precision.HIGHEST
HALF_SHELL = [(step_x, step_y, step_z) for step_x in (-1, 0, 1) for step_y in (-1, 0, 1) for step_z in (-1, 0, 1) if (step_x, step_y, step_z) > (0, 0, 0)]

def pair_terms(target_mid, target_weight, source_mid, source_weight, offset, with_back):
    coupling = jnp.dot(target_weight.T, source_weight, precision=HIGHEST, preferred_element_type=jnp.float32)
    deltas = [target_mid[component][:, None] - source_mid[component][None, :] - float(offset[component]) for component in range(3)]
    squared = deltas[0] * deltas[0] + deltas[1] * deltas[1] + deltas[2] * deltas[2]
    inner_inv = lax.rsqrt(squared + CORE_WIDTH * CORE_WIDTH)
    outer_inv = lax.rsqrt(squared + SPLIT_WIDTH * SPLIT_WIDTH)
    strength = coupling * (inner_inv * inner_inv * inner_inv - outer_inv * outer_inv * outer_inv)
    forward = jnp.stack([lax.optimization_barrier(jnp.sum(strength * delta_part, axis=1)) for delta_part in deltas])
    if with_back:
        backward = -jnp.stack([lax.optimization_barrier(jnp.sum(strength * delta_part, axis=0)) for delta_part in deltas])
        return (forward, backward)
    return forward

def cell_moments(weights, middle, cell_coords):
    offset_rows = [middle[component] + (cell_coords[component] % 2).astype(jnp.float32) - 1.0 for component in range(3)]
    moment_basis = [jnp.ones_like(middle[0])] + offset_rows + [offset_rows[first] * offset_rows[second] for first in range(3) for second in range(3)]
    return jnp.dot(weights, jnp.stack(moment_basis).T, precision=HIGHEST, preferred_element_type=jnp.float32)

def far_field(coarse_table, weights, middle, cell_coords, fine_dims, coarse_dims):
    coarse_count = coarse_dims[0] * coarse_dims[1] * coarse_dims[2]
    coarse_index = jnp.arange(coarse_count, dtype=jnp.int32)
    coarse_coords = (coarse_index // (coarse_dims[1] * coarse_dims[2]), coarse_index // coarse_dims[2] % coarse_dims[1], coarse_index % coarse_dims[2])
    displace = []
    for component in range(3):
        cell_gap = cell_coords[component] - 2 * coarse_coords[component]
        cell_gap = (cell_gap + fine_dims[component] // 2) % fine_dims[component] - fine_dims[component] // 2
        displace.append(cell_gap.astype(jnp.float32)[:, None] + middle[component][None, :] - 1.0)
    spread = jnp.stack(displace)
    weighted = jnp.einsum('kcq,ci->qki', coarse_table.reshape(coarse_count, 9, 13), weights, precision=HIGHEST)
    monopole = weighted[0]
    dipole = weighted[1:4]
    quadrupole = weighted[4:13].reshape(3, 3, coarse_count, weights.shape[1])
    inv_radius = lax.rsqrt(lax.optimization_barrier(jnp.sum(spread * spread, axis=0)) + SPLIT_WIDTH * SPLIT_WIDTH)
    inv_cube = inv_radius * inv_radius * inv_radius
    inv_fifth = inv_cube * inv_radius * inv_radius
    inv_seventh = inv_fifth * inv_radius * inv_radius
    dipole_dot = lax.optimization_barrier(jnp.sum(dipole * spread, axis=0))
    quad_dot = lax.optimization_barrier(jnp.sum(quadrupole * spread[None], axis=1))
    quad_form = lax.optimization_barrier(jnp.sum(spread * quad_dot, axis=0))
    quad_trace = quadrupole[0, 0] + quadrupole[1, 1] + quadrupole[2, 2]
    radial = -monopole * inv_cube - 3.0 * dipole_dot * inv_fifth - 7.5 * quad_form * inv_seventh + 1.5 * quad_trace * inv_fifth
    gradient = spread * radial[None] + dipole * inv_cube[None] + 3.0 * quad_dot * inv_fifth[None]
    return -lax.optimization_barrier(jnp.sum(gradient, axis=1))

def reference(midpoints, line_vectors, burgers, live_mask, pair_list):
    cell_count = NX * NY * NZ
    alive_mask = live_mask.astype(jnp.float32)
    masked_line = line_vectors * alive_mask[None]
    weights = (burgers[:, None] * masked_line[None]).reshape(9, NX, NY, NZ, SEG)

    def to_rows(cell_grid):
        return jnp.moveaxis(cell_grid, 0, 3).reshape(cell_count, cell_grid.shape[0], SEG)

    def to_grid(row_array):
        return jnp.moveaxis(row_array.reshape(NX, NY, NZ, 3, SEG), 3, 0)
    flat_mid = to_rows(midpoints)
    flat_weight = to_rows(weights)
    summed = to_grid(lax.map(lambda record: pair_terms(record[0], record[1], record[0], record[1], (0, 0, 0), False), (flat_mid, flat_weight)))
    for offset_index, offset in enumerate(HALF_SHELL):
        back_shift = (-offset[0], -offset[1], -offset[2])
        source_mid = to_rows(jnp.roll(midpoints, back_shift, axis=(1, 2, 3)))
        source_weight = to_rows(jnp.roll(weights, back_shift, axis=(1, 2, 3)))
        pair_flags = pair_list[offset_index].reshape(cell_count)

        def one_pair(record, offset=offset):
            zeros_block = jnp.zeros((3, SEG), midpoints.dtype)
            return lax.cond(record[4] > 0, lambda: pair_terms(record[0], record[1], record[2], record[3], offset, True), lambda: (zeros_block, zeros_block))
        forward, backward = lax.map(one_pair, (flat_mid, flat_weight, source_mid, source_weight, pair_flags))
        summed = summed + to_grid(forward) + jnp.roll(to_grid(backward), offset, axis=(1, 2, 3))
    grid_ids = jnp.arange(cell_count, dtype=jnp.int32)
    coord_x = grid_ids // (NY * NZ)
    coord_y = grid_ids // NZ % NY
    coord_z = grid_ids % NZ
    moments = lax.map(lambda record: cell_moments(record[0], record[1], (record[2], record[3], record[4])), (flat_weight, flat_mid, coord_x, coord_y, coord_z))
    coarse_table = moments.reshape(NX // 2, 2, NY // 2, 2, NZ // 2, 2, 117).sum(axis=(1, 3, 5)).reshape(-1, 117)
    coarse_dims = (NX // 2, NY // 2, NZ // 2)
    far = lax.map(lambda record: far_field(coarse_table, record[0], record[1], (record[2], record[3], record[4]), (NX, NY, NZ), coarse_dims), (flat_weight, flat_mid, coord_x, coord_y, coord_z))
    return (summed + to_grid(far)) * alive_mask[None]
```

```python
import functools

import jax
import jax.numpy as jnp
from jax import lax
from jax.experimental import pallas as pl
from jax.experimental.pallas import tpu as pltpu
from jax.sharding import PartitionSpec as P

AXES = ("gx", "gy", "gz")
CORE_SQ = 0.1 * 0.1
SPLIT_SQ = 2.0 * 2.0
LANES = 256
ROWS = 512
CHUNK = 256
UNROLL = 4
GRAIN = 128
F32 = jnp.float32
BF16 = jnp.bfloat16
NT = (((1,), (1,)), ((), ()))


def reps(size):
    return [0] if size == 1 else [0, 1] if size == 2 else [0, 1, -1]


def cell_id(cell, dims):
    return (cell[0] * dims[1] + cell[1]) * dims[2] + cell[2]


def gather_kernel(dims, mid_ref, line_ref, burg_ref, live_ref, pair_ref, blocks, ctrl,
                  weights, basis, send_sem, recv_sem, csend_sem, crecv_sem):
    me = tuple(lax.axis_index(a) for a in AXES)
    my_id = cell_id(me, dims)
    count = dims[0] * dims[1] * dims[2]
    barrier = pltpu.get_barrier_semaphore()

    def coords(other):
        return (other // (dims[1] * dims[2]), other // dims[2] % dims[1], other % dims[2])

    def greet(step, carry):
        pl.semaphore_signal(barrier, inc=1, device_id=coords((my_id + step) % count),
                            device_id_type=pl.DeviceIdType.MESH)
        return carry

    lax.fori_loop(1, count, greet, 0)

    alive = live_ref[...].astype(F32)
    line, burg, mid = [], [], []
    for c in range(3):
        mid.append(mid_ref[c])
        line.append(line_ref[c] * alive)
        burg.append(burg_ref[c])
        blocks[0, c] = mid[c]
        blocks[0, 3 + c] = line[c]
        blocks[0, 6 + c] = burg[c]
    basis[...] = jnp.zeros_like(basis)
    weights[...] = jnp.zeros_like(weights)
    z = [mid[c] + ((me[c] % 2) - 1).astype(F32) for c in range(3)]
    rows = [jnp.ones_like(z[0])] + z + [z[a] * z[b] for a in range(3) for b in range(3)]
    for q in range(13):
        basis[q:q + 1] = rows[q]
    for a in range(3):
        for b in range(3):
            weights[3 * a + b:3 * a + b + 1] = burg[a] * line[b]
    moments = lax.dot_general(weights[...], basis[...], NT, precision=lax.Precision.HIGHEST,
                              preferred_element_type=F32)
    sub = lax.broadcasted_iota(jnp.int32, moments.shape, 0)
    flat = jnp.where(sub == 0, moments, 0.0)
    for c in range(1, 9):
        flat = flat + pltpu.roll(jnp.where(sub == c, moments, 0.0), 13 * c, 1)
    ctrl[my_id, 0:1] = jnp.sum(flat, axis=0, keepdims=True)
    lane = lax.broadcasted_iota(jnp.int32, (1, 128), 1)
    flags = jnp.where(lane == 13, jnp.sum(alive, axis=1, keepdims=True), 0.0)
    for k in range(13):
        flags = flags + jnp.where(lane == k, pair_ref[k].astype(F32), 0.0)
    ctrl[my_id, 1:2] = flags

    pl.semaphore_wait(barrier, count - 1)

    grid = [(x, y, w) for x in reps(dims[0]) for y in reps(dims[1]) for w in reps(dims[2])]
    copies = []
    for slot, rep in enumerate(grid):
        if slot == 0:
            continue
        to = tuple((me[i] - rep[i] + dims[i]) % dims[i] for i in range(3))
        copy = pltpu.make_async_remote_copy(
            src_ref=blocks.at[0], dst_ref=blocks.at[slot], send_sem=send_sem.at[slot],
            recv_sem=recv_sem.at[slot], device_id=to, device_id_type=pl.DeviceIdType.MESH)
        copy.start()
        copies.append(copy)

    def ctrl_copy(step):
        return pltpu.make_async_remote_copy(
            src_ref=ctrl.at[my_id], dst_ref=ctrl.at[my_id], send_sem=csend_sem.at[step],
            recv_sem=crecv_sem.at[step], device_id=coords((my_id + step) % count),
            device_id_type=pl.DeviceIdType.MESH)

    def send_ctrl(step, carry):
        ctrl_copy(step).start()
        return carry

    lax.fori_loop(1, count, send_ctrl, 0)

    def wait_ctrl(step, carry):
        ctrl_copy(step).wait()
        return carry

    lax.fori_loop(1, count, wait_ctrl, 0)
    for copy in copies:
        copy.wait()


def split3(value):
    high = value.astype(BF16).astype(F32)
    rest = value - high
    middle = rest.astype(BF16).astype(F32)
    return high, middle, rest - middle


def force_kernel(dims, scalars, blocks, ctrl, mid8, line8, burg8, live8, out,
                 feat, wide, tall, held, rows, cols, high0, low0, high1, low1, acc,
                 coarse, coarse_s, sem):
    me = tuple(lax.axis_index(a) for a in AXES)
    my_id = cell_id(me, dims)
    seg = blocks.shape[3]
    kdims = tuple(d // 2 for d in dims)
    kcount = kdims[0] * kdims[1] * kdims[2]
    tiles = seg // LANES

    def coarse_sum(k, carry):
        kx, ky, kz = k // (kdims[1] * kdims[2]), k // kdims[2] % kdims[1], k % kdims[2]
        total = jnp.zeros((1, 128), F32)
        for a in range(2):
            for b in range(2):
                for c in range(2):
                    total = total + ctrl[cell_id((2 * kx + a, 2 * ky + b, 2 * kz + c), dims), 0:1]
        coarse[k] = total
        return carry

    lax.fori_loop(0, kcount, coarse_sum, 0)
    table = pltpu.make_async_copy(coarse, coarse_s, sem)
    table.start()

    feat[...] = jnp.zeros_like(feat)
    wide[...] = jnp.zeros_like(wide)
    tall[...] = jnp.zeros_like(tall)
    held[...] = jnp.zeros_like(held)
    acc[...] = jnp.zeros_like(acc)
    for buf in (high0, low0, high1, low1):
        buf[...] = jnp.zeros_like(buf)

    def fill_weights(slot):
        for a in range(3):
            for b in range(3):
                wide[3 * a + b:3 * a + b + 1] = blocks[slot, 6 + a] * blocks[slot, 3 + b]
        whole = wide[...]
        whigh = whole.astype(BF16).astype(F32)
        return whigh, whole - whigh

    ones = jnp.ones((1, seg), F32)
    x = [blocks[0, c] - 0.5 for c in range(3)]
    for c in range(3):
        feat[c:c + 1] = -2.0 * x[c]
    feat[3:4] = ones
    feat[4:5] = x[0] * x[0] + x[1] * x[1] + x[2] * x[2] + CORE_SQ
    high, middle, low = split3(feat[...])
    whigh, wlow = fill_weights(0)
    distance = jnp.concatenate([high, high, high, middle, middle, low], axis=0).astype(BF16)
    coupling = jnp.concatenate([whigh, whigh, wlow], axis=0).astype(BF16)
    for t in range(tiles):
        cut = slice(t * LANES, (t + 1) * LANES)
        held[0:48, 2 * t * LANES:(2 * t + 1) * LANES] = distance[:, cut]
        held[48:96, (2 * t + 1) * LANES:(2 * t + 2) * LANES] = coupling[:, cut]

    def slot_of(offset):
        slot = 0
        for i in range(3):
            base = min(dims[i], 3)
            slot = slot * base + (offset[i] + base) % base
        return slot

    def append_source(t, at):
        offset = (t // 9 - 1, t // 3 % 3 - 1, t % 3 - 1)
        source_id = cell_id(tuple((me[i] + offset[i] + dims[i]) % dims[i] for i in range(3)), dims)
        ahead = t > 13
        flag = scalars[jnp.where(ahead, my_id, source_id), 1,
                       jnp.where(ahead, t - 14, jnp.maximum(12 - t, 0))]
        listed = jnp.logical_or(t == 13, flag > 0.0)

        @pl.when(listed)
        def _():
            slot = slot_of(offset)
            y = [blocks[slot, c] + (offset[c].astype(F32) - 0.5) for c in range(3)]
            for c in range(3):
                feat[c:c + 1] = y[c]
            feat[3:4] = y[0] * y[0] + y[1] * y[1] + y[2] * y[2]
            feat[4:5] = ones
            high, middle, low = split3(feat[...])
            for k, part in enumerate((high, middle, low, high, middle, high)):
                tall[8 * k:8 * k + 8] = part
            whigh, wlow = fill_weights(slot)
            tall[48:64] = whigh
            tall[64:80] = wlow
            tall[80:96] = whigh
            rows[pl.ds(pl.multiple_of(at, GRAIN), seg), :] = jnp.transpose(tall[...]).astype(BF16)
            cols[:, pl.ds(pl.multiple_of(at, GRAIN), seg)] = jnp.concatenate(
                [high, middle + pltpu.roll(low, 4, 0)], axis=0).astype(BF16)

        size = (scalars[source_id, 1, 13].astype(jnp.int32) + (GRAIN - 1)) // GRAIN * GRAIN
        return at + jnp.where(listed, size, 0)

    total = lax.fori_loop(0, 27, append_source, 0)
    lane = lax.broadcasted_iota(jnp.int32, (ROWS, 128), 1)
    rows[pl.ds(pl.multiple_of(total, GRAIN), ROWS), :] = (lane == 3).astype(F32).astype(BF16)
    cols[:, pl.ds(pl.multiple_of(total, GRAIN), ROWS)] = jnp.zeros((16, ROWS), BF16)

    my_tiles = (scalars[my_id, 1, 13].astype(jnp.int32) + (LANES - 1)) // LANES
    spans = (total + (ROWS - 1)) // ROWS
    steps = my_tiles * spans
    buffers = ((high0, low0), (high1, low1))

    def place(step):
        done = step >= steps
        tile = jnp.where(done, tiles, step // spans)
        return tile, jnp.where(done, 0, step % spans)

    def strengths(step, to):
        tile, span = place(step)
        w = held[:, pl.ds(pl.multiple_of(tile * (2 * LANES), 2 * LANES), 2 * LANES)]
        for u in range(0, ROWS, CHUNK):
            lhs = rows[pl.ds(pl.multiple_of(span * ROWS + u, CHUNK), CHUNK), :]
            product = jnp.dot(lhs, w, preferred_element_type=F32)
            near, pull = product[:, :LANES], product[:, LANES:]
            inner = lax.rsqrt(near)
            outer = lax.rsqrt(near + (SPLIT_SQ - CORE_SQ))
            strength = pull * (inner * inner * inner - outer * outer * outer)
            top = strength.astype(BF16)
            to[0][u:u + CHUNK] = top
            to[1][u:u + CHUNK] = (strength - top.astype(F32)).astype(BF16)

    def gather_force(step, of):
        tile, span = place(step)
        part = cols[:, pl.ds(pl.multiple_of(span * ROWS, ROWS), ROWS)]
        acc[tile] += (jnp.dot(part, of[0][...], preferred_element_type=F32)
                      + jnp.dot(part, of[1][...], preferred_element_type=F32))

    def some_steps(i, carry):
        for k in range(UNROLL):
            step = i * UNROLL + k
            strengths(step, buffers[k % 2])
            gather_force(jnp.maximum(step - 1, 0), buffers[1 - k % 2])
        return carry

    groups = (steps + (UNROLL - 1)) // UNROLL
    lax.fori_loop(0, groups, some_steps, 0)
    gather_force(groups * UNROLL - 1, buffers[1])

    table.wait()
    alive = live8[...].astype(F32)
    w8 = [burg8[a] * (line8[b] * alive) for a in range(3) for b in range(3)]

    def far_step(k, grads):
        kc = (k // (kdims[1] * kdims[2]), k // kdims[2] % kdims[1], k % kdims[2])
        u = []
        for i in range(3):
            gap = (me[i] - 2 * kc[i] + dims[i] + dims[i] // 2) % dims[i] - dims[i] // 2
            u.append(mid8[i] + (gap.astype(F32) - 1.0))
        q = []
        for m in range(13):
            value = coarse_s[k, 0, m] * w8[0]
            for c in range(1, 9):
                value = value + coarse_s[k, 0, 13 * c + m] * w8[c]
            q.append(value)
        inv = lax.rsqrt(u[0] * u[0] + u[1] * u[1] + u[2] * u[2] + SPLIT_SQ)
        inv2 = inv * inv
        inv3 = inv2 * inv
        inv5 = inv3 * inv2
        inv7 = inv5 * inv2
        dip = q[1] * u[0] + q[2] * u[1] + q[3] * u[2]
        quad = [q[4 + 3 * a] * u[0] + q[5 + 3 * a] * u[1] + q[6 + 3 * a] * u[2] for a in range(3)]
        form = quad[0] * u[0] + quad[1] * u[1] + quad[2] * u[2]
        trace = q[4] + q[8] + q[12]
        radial = (1.5 * trace - 3.0 * dip) * inv5 - q[0] * inv3 - 7.5 * form * inv7
        return tuple(grads[c] + u[c] * radial + q[1 + c] * inv3 + 3.0 * quad[c] * inv5
                     for c in range(3))

    width = seg // 8
    zero = jnp.zeros((8, width), F32)
    grads = lax.fori_loop(0, kcount, far_step, (zero, zero, zero))
    for c in range(3):
        for t in range(tiles):
            turned = acc[t]
            cut = slice(t * LANES, (t + 1) * LANES)
            near = x[c][:, cut] * turned[4:5] - (turned[c:c + 1] + turned[8 + c:9 + c] + turned[12 + c:13 + c])
            for s in range(t * LANES // width, (t + 1) * LANES // width):
                inside = slice(s * width - t * LANES, (s + 1) * width - t * LANES)
                out[c, :, s * width:(s + 1) * width] = (near[:, inside] - grads[c][s:s + 1]) * alive[s:s + 1]


def on_device(dims, midpoints, line_vectors, burgers, live_mask, pair_list):
    seg = midpoints.shape[4]
    count = dims[0] * dims[1] * dims[2]
    kcount = count // 8
    slots = len(reps(dims[0])) * len(reps(dims[1])) * len(reps(dims[2]))
    mid, line, burg = (a.reshape(3, 1, seg) for a in (midpoints, line_vectors, burgers))
    vmem = pl.BlockSpec(memory_space=pltpu.VMEM)
    smem = pl.BlockSpec(memory_space=pltpu.SMEM)
    blocks, ctrl = pl.pallas_call(
        functools.partial(gather_kernel, dims),
        out_shape=(jax.ShapeDtypeStruct((slots, 9, 1, seg), F32),
                   jax.ShapeDtypeStruct((count, 2, 128), F32)),
        in_specs=[vmem] * 5,
        out_specs=(vmem, vmem),
        scratch_shapes=[
            pltpu.VMEM((16, seg), F32),
            pltpu.VMEM((128, seg), F32),
            pltpu.SemaphoreType.DMA((slots,)),
            pltpu.SemaphoreType.DMA((slots,)),
            pltpu.SemaphoreType.DMA((count,)),
            pltpu.SemaphoreType.DMA((count,)),
        ],
        compiler_params=pltpu.CompilerParams(collective_id=0, has_side_effects=True),
        name="gather",
    )(mid, line, burg, live_mask.reshape(1, seg), pair_list.reshape(13, 1, 1))
    eight = [a.reshape(3, 8, seg // 8) for a in (midpoints, line_vectors, burgers)]
    out = pl.pallas_call(
        functools.partial(force_kernel, dims),
        out_shape=jax.ShapeDtypeStruct((3, 1, seg), F32),
        in_specs=[smem] + [vmem] * 6,
        out_specs=vmem,
        scratch_shapes=[
            pltpu.VMEM((8, seg), F32),
            pltpu.VMEM((16, seg), F32),
            pltpu.VMEM((128, seg), F32),
            pltpu.VMEM((128, 2 * seg + 2 * LANES), BF16),
            pltpu.VMEM((27 * seg + ROWS, 128), BF16),
            pltpu.VMEM((16, 27 * seg + ROWS), BF16),
            pltpu.VMEM((ROWS, LANES), BF16),
            pltpu.VMEM((ROWS, LANES), BF16),
            pltpu.VMEM((ROWS, LANES), BF16),
            pltpu.VMEM((ROWS, LANES), BF16),
            pltpu.VMEM((seg // LANES + 1, 16, LANES), F32),
            pltpu.VMEM((kcount, 1, 128), F32),
            pltpu.SMEM((kcount, 1, 128), F32),
            pltpu.SemaphoreType.DMA,
        ],
        compiler_params=pltpu.CompilerParams(vmem_limit_bytes=48 * 2**20),
        name="forces",
    )(ctrl, blocks, ctrl, *eight, live_mask.reshape(8, seg // 8))
    return out.reshape(3, 1, 1, 1, seg)


def solution(mesh):
    dims = tuple(mesh.shape[a] for a in AXES)
    placed = (
        P(None, "gx", "gy", "gz", None),
        P(None, "gx", "gy", "gz", None),
        P(None, "gx", "gy", "gz", None),
        P("gx", "gy", "gz", None),
        P(None, "gx", "gy", "gz"),
    )
    return jax.shard_map(
        functools.partial(on_device, dims),
        mesh=mesh,
        in_specs=placed,
        out_specs=P(None, "gx", "gy", "gz", None),
        check_vma=False,
    )
```

```python
import functools

import jax
import jax.numpy as jnp
from jax import lax
from jax.experimental import pallas as pl
from jax.experimental.pallas import tpu as pltpu
from jax.sharding import PartitionSpec as P

AXES = ("gx", "gy", "gz")
CORE_SQ = 0.1 * 0.1
SPLIT_SQ = 2.0 * 2.0
LANES = 256
ROWS = 512
CHUNK = 256
UNROLL = 4
GRAIN = 128
F32 = jnp.float32
BF16 = jnp.bfloat16
NT = (((1,), (1,)), ((), ()))


def reps(size):
    return [0] if size == 1 else [0, 1] if size == 2 else [0, 1, -1]


def cell_id(cell, dims):
    return (cell[0] * dims[1] + cell[1]) * dims[2] + cell[2]


def slot_index(dims, rep):
    slot = 0
    for i in range(3):
        base = min(dims[i], 3)
        slot = slot * base + (rep[i] + base) % base
    return slot


def gather_kernel(dims, mid_ref, line_ref, burg_ref, live_ref, pair_ref, blocks, ctrl, table,
                  weights, basis, sums, send_sem, recv_sem, part_send, part_recv, table_send, table_recv):
    me = tuple(lax.axis_index(a) for a in AXES)
    seg = mid_ref.shape[2]
    kdims = tuple(d // 2 for d in dims)
    kcount = kdims[0] * kdims[1] * kdims[2]
    my_coarse = cell_id(tuple(me[i] // 2 for i in range(3)), kdims)
    barrier = pltpu.get_barrier_semaphore()
    mesh_id = pl.DeviceIdType.MESH

    def at(rep):
        return tuple((me[i] - rep[i] + dims[i]) % dims[i] for i in range(3))

    def peer(step):
        other = (my_coarse + step) % kcount
        coarse = (other // (kdims[1] * kdims[2]), other // kdims[2] % kdims[1], other % kdims[2])
        return tuple(2 * coarse[i] + me[i] % 2 for i in range(3))

    steps = [tuple(r if i == axis else 0 for i in range(3))
             for axis in range(3) for r in reps(dims[axis]) if r != 0]
    for rep in steps:
        pl.semaphore_signal(barrier, inc=1, device_id=at(rep), device_id_type=mesh_id)

    def greet(step, carry):
        pl.semaphore_signal(barrier, inc=1, device_id=peer(step), device_id_type=mesh_id)
        return carry

    lax.fori_loop(1, kcount, greet, 0)

    alive = live_ref[...].astype(F32)
    line, burg, mid = [], [], []
    for c in range(3):
        mid.append(mid_ref[c])
        line.append(line_ref[c] * alive)
        burg.append(burg_ref[c])
        blocks[0, :, c * seg:(c + 1) * seg] = mid[c]
        blocks[0, :, (3 + c) * seg:(4 + c) * seg] = line[c]
        blocks[0, :, (6 + c) * seg:(7 + c) * seg] = burg[c]
    lane = lax.broadcasted_iota(jnp.int32, (1, 128), 1)
    blocks[0, :, 9 * seg:9 * seg + 128] = jnp.where(lane == 13, jnp.sum(alive, axis=1, keepdims=True), 0.0)
    blocks[0, :, 9 * seg:9 * seg + 13] = pair_ref[...].astype(F32)

    pl.semaphore_wait(barrier, len(steps) + kcount - 1)

    copies = {}

    def send(rep, axis):
        kept = tuple(0 if i == axis else rep[i] for i in range(3))
        moved = tuple(rep[i] if i == axis else 0 for i in range(3))
        slot = slot_index(dims, rep)
        copy = pltpu.make_async_remote_copy(
            src_ref=blocks.at[slot_index(dims, kept)], dst_ref=blocks.at[slot],
            send_sem=send_sem.at[slot], recv_sem=recv_sem.at[slot],
            device_id=at(moved), device_id_type=mesh_id)
        copy.start()
        copies[slot] = copy

    def arrived(rep):
        copies[slot_index(dims, rep)].wait_recv()

    xs, ys, zs = (reps(d)[1:] for d in dims)
    for r in zs:
        send((0, 0, r), 2)
    for r in xs:
        send((r, 0, 0), 0)
    for r in ys:
        send((0, r, 0), 1)

    basis[...] = jnp.zeros_like(basis)
    weights[...] = jnp.zeros_like(weights)
    z = [mid[c] + ((me[c] % 2) - 1).astype(F32) for c in range(3)]
    rows = [jnp.ones_like(z[0])] + z + [z[a] * z[b] for a in range(3) for b in range(3)]
    for q in range(13):
        basis[q:q + 1] = rows[q]
    for a in range(3):
        for b in range(3):
            weights[3 * a + b:3 * a + b + 1] = burg[a] * line[b]
    moments = lax.dot_general(weights[...], basis[...], NT, precision=lax.Precision.HIGHEST,
                              preferred_element_type=F32)
    sub = lax.broadcasted_iota(jnp.int32, moments.shape, 0)
    flat = jnp.where(sub == 0, moments, 0.0)
    for c in range(1, 9):
        flat = flat + pltpu.roll(jnp.where(sub == c, moments, 0.0), 13 * c, 1)
    sums[0] = jnp.sum(flat, axis=0, keepdims=True)

    def part_copy(axis):
        partner = tuple(me[i] + 1 - 2 * (me[i] % 2) if i == axis else me[i] for i in range(3))
        return pltpu.make_async_remote_copy(
            src_ref=sums.at[axis], dst_ref=sums.at[4 + axis], send_sem=part_send.at[axis],
            recv_sem=part_recv.at[axis], device_id=partner, device_id_type=mesh_id)

    def finish_part(axis):
        part_copy(axis).wait_recv()
        sums[axis + 1] = sums[axis] + sums[4 + axis]

    part_copy(0).start()
    for r in zs:
        arrived((0, 0, r))
        for a in xs:
            send((a, 0, r), 0)
        for b in ys:
            send((0, b, r), 1)
    for a in xs:
        arrived((a, 0, 0))
        for b in ys:
            send((a, b, 0), 1)
    finish_part(0)
    part_copy(1).start()
    for r in zs:
        for a in xs:
            arrived((a, 0, r))
            for b in ys:
                send((a, b, r), 1)
    finish_part(1)
    part_copy(2).start()
    finish_part(2)
    table[my_coarse] = sums[3]

    def table_copy(step):
        return pltpu.make_async_remote_copy(
            src_ref=table.at[my_coarse], dst_ref=table.at[my_coarse], send_sem=table_send.at[step],
            recv_sem=table_recv.at[step], device_id=peer(step), device_id_type=mesh_id)

    def start_table(step, carry):
        table_copy(step).start()
        return carry

    lax.fori_loop(1, kcount, start_table, 0)
    for rep in [(a, b, r) for r in [0] + zs for a in [0] + xs for b in ys]:
        arrived(rep)

    def wait_table(step, carry):
        table_copy(step).wait()
        return carry

    lax.fori_loop(1, kcount, wait_table, 0)
    for axis in range(3):
        part_copy(axis).wait_send()
    for copy in copies.values():
        copy.wait_send()
    for slot in range(blocks.shape[0]):
        ctrl[slot] = blocks[slot, :, 9 * seg:9 * seg + 128]


def split3(value):
    high = value.astype(BF16).astype(F32)
    rest = value - high
    middle = rest.astype(BF16).astype(F32)
    return high, middle, rest - middle


def force_kernel(dims, scalars, table, blocks, mid8, line8, burg8, live8, out,
                 feat, wide, tall, held, rows, cols, high0, low0, high1, low1, acc):
    me = tuple(lax.axis_index(a) for a in AXES)
    seg = held.shape[1] // 2 - LANES
    kdims = tuple(d // 2 for d in dims)
    kcount = kdims[0] * kdims[1] * kdims[2]
    tiles = seg // LANES

    feat[...] = jnp.zeros_like(feat)
    wide[...] = jnp.zeros_like(wide)
    tall[...] = jnp.zeros_like(tall)
    held[...] = jnp.zeros_like(held)
    acc[...] = jnp.zeros_like(acc)
    for buf in (high0, low0, high1, low1):
        buf[...] = jnp.zeros_like(buf)

    def row(slot, c):
        return blocks[slot, :, c * seg:(c + 1) * seg]

    def fill_weights(slot):
        for a in range(3):
            for b in range(3):
                wide[3 * a + b:3 * a + b + 1] = row(slot, 6 + a) * row(slot, 3 + b)
        whole = wide[...]
        whigh = whole.astype(BF16).astype(F32)
        return whigh, whole - whigh

    ones = jnp.ones((1, seg), F32)
    x = [row(0, c) - 0.5 for c in range(3)]
    for c in range(3):
        feat[c:c + 1] = -2.0 * x[c]
    feat[3:4] = ones
    feat[4:5] = x[0] * x[0] + x[1] * x[1] + x[2] * x[2] + CORE_SQ
    high, middle, low = split3(feat[...])
    whigh, wlow = fill_weights(0)
    distance = jnp.concatenate([high, high, high, middle, middle, low], axis=0).astype(BF16)
    coupling = jnp.concatenate([whigh, whigh, wlow], axis=0).astype(BF16)
    for t in range(tiles):
        cut = slice(t * LANES, (t + 1) * LANES)
        held[0:48, 2 * t * LANES:(2 * t + 1) * LANES] = distance[:, cut]
        held[48:96, (2 * t + 1) * LANES:(2 * t + 2) * LANES] = coupling[:, cut]

    def append_source(t, at):
        offset = (t // 9 - 1, t // 3 % 3 - 1, t % 3 - 1)
        slot = slot_index(dims, offset)
        ahead = t > 13
        flag = scalars[jnp.where(ahead, 0, slot), 0,
                       jnp.where(ahead, t - 14, jnp.maximum(12 - t, 0))]
        listed = jnp.logical_or(t == 13, flag > 0.0)

        @pl.when(listed)
        def _():
            y = [row(slot, c) + (offset[c].astype(F32) - 0.5) for c in range(3)]
            for c in range(3):
                feat[c:c + 1] = y[c]
            feat[3:4] = y[0] * y[0] + y[1] * y[1] + y[2] * y[2]
            feat[4:5] = ones
            high, middle, low = split3(feat[...])
            for k, part in enumerate((high, middle, low, high, middle, high)):
                tall[8 * k:8 * k + 8] = part
            whigh, wlow = fill_weights(slot)
            tall[48:64] = whigh
            tall[64:80] = wlow
            tall[80:96] = whigh
            rows[pl.ds(pl.multiple_of(at, GRAIN), seg), :] = jnp.transpose(tall[...]).astype(BF16)
            cols[:, pl.ds(pl.multiple_of(at, GRAIN), seg)] = jnp.concatenate(
                [high, middle + pltpu.roll(low, 4, 0)], axis=0).astype(BF16)

        size = (scalars[slot, 0, 13].astype(jnp.int32) + (GRAIN - 1)) // GRAIN * GRAIN
        return at + jnp.where(listed, size, 0)

    total = lax.fori_loop(0, 27, append_source, 0)
    lane = lax.broadcasted_iota(jnp.int32, (ROWS, 128), 1)
    rows[pl.ds(pl.multiple_of(total, GRAIN), ROWS), :] = (lane == 3).astype(F32).astype(BF16)
    cols[:, pl.ds(pl.multiple_of(total, GRAIN), ROWS)] = jnp.zeros((16, ROWS), BF16)

    my_tiles = (scalars[0, 0, 13].astype(jnp.int32) + (LANES - 1)) // LANES
    spans = (total + (ROWS - 1)) // ROWS
    steps = my_tiles * spans
    buffers = ((high0, low0), (high1, low1))

    def place(step):
        done = step >= steps
        tile = jnp.where(done, tiles, step // spans)
        return tile, jnp.where(done, 0, step % spans)

    def strengths(step, to):
        tile, span = place(step)
        w = held[:, pl.ds(pl.multiple_of(tile * (2 * LANES), 2 * LANES), 2 * LANES)]
        for u in range(0, ROWS, CHUNK):
            lhs = rows[pl.ds(pl.multiple_of(span * ROWS + u, CHUNK), CHUNK), :]
            product = jnp.dot(lhs, w, preferred_element_type=F32)
            near, pull = product[:, :LANES], product[:, LANES:]
            inner = lax.rsqrt(near)
            outer = lax.rsqrt(near + (SPLIT_SQ - CORE_SQ))
            strength = pull * (inner * inner * inner - outer * outer * outer)
            top = strength.astype(BF16)
            to[0][u:u + CHUNK] = top
            to[1][u:u + CHUNK] = (strength - top.astype(F32)).astype(BF16)

    def gather_force(step, of):
        tile, span = place(step)
        part = cols[:, pl.ds(pl.multiple_of(span * ROWS, ROWS), ROWS)]
        acc[tile] += (jnp.dot(part, of[0][...], preferred_element_type=F32)
                      + jnp.dot(part, of[1][...], preferred_element_type=F32))

    def some_steps(i, carry):
        for k in range(UNROLL):
            step = i * UNROLL + k
            strengths(step, buffers[k % 2])
            gather_force(jnp.maximum(step - 1, 0), buffers[1 - k % 2])
        return carry

    groups = (steps + (UNROLL - 1)) // UNROLL
    lax.fori_loop(0, groups, some_steps, 0)
    gather_force(groups * UNROLL - 1, buffers[1])

    alive = live8[...].astype(F32)
    w8 = [burg8[a] * (line8[b] * alive) for a in range(3) for b in range(3)]

    def far_step(k, grads):
        kc = (k // (kdims[1] * kdims[2]), k // kdims[2] % kdims[1], k % kdims[2])
        u = []
        for i in range(3):
            gap = (me[i] - 2 * kc[i] + dims[i] + dims[i] // 2) % dims[i] - dims[i] // 2
            u.append(mid8[i] + (gap.astype(F32) - 1.0))
        q = []
        for m in range(13):
            value = table[k, 0, m] * w8[0]
            for c in range(1, 9):
                value = value + table[k, 0, 13 * c + m] * w8[c]
            q.append(value)
        inv = lax.rsqrt(u[0] * u[0] + u[1] * u[1] + u[2] * u[2] + SPLIT_SQ)
        inv2 = inv * inv
        inv3 = inv2 * inv
        inv5 = inv3 * inv2
        inv7 = inv5 * inv2
        dip = q[1] * u[0] + q[2] * u[1] + q[3] * u[2]
        quad = [q[4 + 3 * a] * u[0] + q[5 + 3 * a] * u[1] + q[6 + 3 * a] * u[2] for a in range(3)]
        form = quad[0] * u[0] + quad[1] * u[1] + quad[2] * u[2]
        trace = q[4] + q[8] + q[12]
        radial = (1.5 * trace - 3.0 * dip) * inv5 - q[0] * inv3 - 7.5 * form * inv7
        return tuple(grads[c] + u[c] * radial + q[1 + c] * inv3 + 3.0 * quad[c] * inv5
                     for c in range(3))

    width = seg // 8
    zero = jnp.zeros((8, width), F32)
    grads = lax.fori_loop(0, kcount, far_step, (zero, zero, zero))
    for c in range(3):
        for t in range(tiles):
            turned = acc[t]
            cut = slice(t * LANES, (t + 1) * LANES)
            near = x[c][:, cut] * turned[4:5] - (turned[c:c + 1] + turned[8 + c:9 + c] + turned[12 + c:13 + c])
            for s in range(t * LANES // width, (t + 1) * LANES // width):
                inside = slice(s * width - t * LANES, (s + 1) * width - t * LANES)
                out[c, :, s * width:(s + 1) * width] = (near[:, inside] - grads[c][s:s + 1]) * alive[s:s + 1]


def on_device(dims, midpoints, line_vectors, burgers, live_mask, pair_list):
    seg = midpoints.shape[4]
    count = dims[0] * dims[1] * dims[2]
    kcount = count // 8
    slots = len(reps(dims[0])) * len(reps(dims[1])) * len(reps(dims[2]))
    mid, line, burg = (a.reshape(3, 1, seg) for a in (midpoints, line_vectors, burgers))
    vmem = pl.BlockSpec(memory_space=pltpu.VMEM)
    smem = pl.BlockSpec(memory_space=pltpu.SMEM)
    blocks, ctrl, table = pl.pallas_call(
        functools.partial(gather_kernel, dims),
        out_shape=(jax.ShapeDtypeStruct((slots, 1, 9 * seg + 128), F32),
                   jax.ShapeDtypeStruct((slots, 1, 128), F32),
                   jax.ShapeDtypeStruct((kcount, 1, 128), F32)),
        in_specs=[vmem] * 5,
        out_specs=(vmem, vmem, vmem),
        scratch_shapes=[
            pltpu.VMEM((16, seg), F32),
            pltpu.VMEM((128, seg), F32),
            pltpu.VMEM((7, 1, 128), F32),
            pltpu.SemaphoreType.DMA((slots,)),
            pltpu.SemaphoreType.DMA((slots,)),
            pltpu.SemaphoreType.DMA((3,)),
            pltpu.SemaphoreType.DMA((3,)),
            pltpu.SemaphoreType.DMA((kcount,)),
            pltpu.SemaphoreType.DMA((kcount,)),
        ],
        compiler_params=pltpu.CompilerParams(collective_id=0, has_side_effects=True),
        name="gather",
    )(mid, line, burg, live_mask.reshape(1, seg), pair_list.reshape(1, 13))
    eight = [a.reshape(3, 8, seg // 8) for a in (midpoints, line_vectors, burgers)]
    out = pl.pallas_call(
        functools.partial(force_kernel, dims),
        out_shape=jax.ShapeDtypeStruct((3, 1, seg), F32),
        in_specs=[smem] * 2 + [vmem] * 5,
        out_specs=vmem,
        scratch_shapes=[
            pltpu.VMEM((8, seg), F32),
            pltpu.VMEM((16, seg), F32),
            pltpu.VMEM((128, seg), F32),
            pltpu.VMEM((128, 2 * seg + 2 * LANES), BF16),
            pltpu.VMEM((27 * seg + ROWS, 128), BF16),
            pltpu.VMEM((16, 27 * seg + ROWS), BF16),
            pltpu.VMEM((ROWS, LANES), BF16),
            pltpu.VMEM((ROWS, LANES), BF16),
            pltpu.VMEM((ROWS, LANES), BF16),
            pltpu.VMEM((ROWS, LANES), BF16),
            pltpu.VMEM((seg // LANES + 1, 16, LANES), F32),
        ],
        compiler_params=pltpu.CompilerParams(vmem_limit_bytes=60 * 2**20),
        name="forces",
    )(ctrl, table, blocks, *eight, live_mask.reshape(8, seg // 8))
    return out.reshape(3, 1, 1, 1, seg)


def solution(mesh):
    dims = tuple(mesh.shape[a] for a in AXES)
    placed = (
        P(None, "gx", "gy", "gz", None),
        P(None, "gx", "gy", "gz", None),
        P(None, "gx", "gy", "gz", None),
        P("gx", "gy", "gz", None),
        P(None, "gx", "gy", "gz"),
    )
    return jax.shard_map(
        functools.partial(on_device, dims),
        mesh=mesh,
        in_specs=placed,
        out_specs=P(None, "gx", "gy", "gz", None),
        check_vma=False,
    )
```

```python
import functools

import jax
import jax.numpy as jnp
from jax import lax
from jax.experimental import pallas as pl
from jax.experimental.pallas import tpu as pltpu
from jax.sharding import PartitionSpec as P

AXES = ("gx", "gy", "gz")
CORE_SQ = 0.1 * 0.1
SPLIT_SQ = 2.0 * 2.0
LANES = 256
ROWS = 512
CHUNK = 256
UNROLL = 8
PARTS = LANES // 128
GRAIN = 128
F32 = jnp.float32
BF16 = jnp.bfloat16
NT = (((1,), (1,)), ((), ()))


def reps(size):
    return [0] if size == 1 else [0, 1] if size == 2 else [0, 1, -1]


def cell_id(cell, dims):
    return (cell[0] * dims[1] + cell[1]) * dims[2] + cell[2]


def split3(value):
    high = value.astype(BF16).astype(F32)
    rest = value - high
    middle = rest.astype(BF16).astype(F32)
    return high, middle, rest - middle


def split_coupling(row, wide):
    for a in range(3):
        for b in range(3):
            wide[3 * a + b:3 * a + b + 1] = row(6 + a) * row(3 + b)
    whole = wide[...]
    high = whole.astype(BF16).astype(F32)
    return high, whole - high


def hold_targets(row, x, feat, wide, held):
    for c in range(3):
        feat[c:c + 1] = -2.0 * x[c]
    feat[3:4] = jnp.ones_like(x[0])
    feat[4:5] = x[0] * x[0] + x[1] * x[1] + x[2] * x[2] + CORE_SQ
    high, middle, low = split3(feat[...])
    whigh, wlow = split_coupling(row, wide)
    distance = jnp.concatenate([high, high, high, middle, middle, low], axis=0).astype(BF16)
    coupling = jnp.concatenate([whigh, whigh, wlow], axis=0).astype(BF16)
    for t in range(held.shape[0] - 1):
        for i in range(PARTS):
            cut = slice(t * LANES + i * 128, t * LANES + (i + 1) * 128)
            held[t, i, 0:48] = distance[:, cut]
            held[t, PARTS + i, 48:96] = coupling[:, cut]


def lay_sources(row, y, feat, wide, tall):
    for c in range(3):
        feat[c:c + 1] = y[c]
    feat[3:4] = y[0] * y[0] + y[1] * y[1] + y[2] * y[2]
    feat[4:5] = jnp.ones_like(y[0])
    high, middle, low = split3(feat[...])
    for k, part in enumerate((high, middle, low, high, middle, high)):
        tall[8 * k:8 * k + 8] = part
    whigh, wlow = split_coupling(row, wide)
    tall[48:64] = whigh
    tall[64:80] = wlow
    tall[80:96] = whigh
    return (jnp.transpose(tall[...]).astype(BF16),
            jnp.concatenate([high, middle + pltpu.roll(low, 4, 0)], axis=0).astype(BF16))


def strengths(held, rows, tile, span, to):
    w = jnp.concatenate([held[tile, i] for i in range(2 * PARTS)], axis=1)
    for u in range(0, ROWS, CHUNK):
        lhs = rows[pl.ds(pl.multiple_of(span * ROWS + u, CHUNK), CHUNK), :]
        product = jnp.dot(lhs, w, preferred_element_type=F32)
        for i in range(PARTS):
            near = product[:, i * 128:(i + 1) * 128]
            pull = product[:, LANES + i * 128:LANES + (i + 1) * 128]
            inner = lax.rsqrt(near)
            outer = lax.rsqrt(near + (SPLIT_SQ - CORE_SQ))
            strength = pull * (inner * inner * inner - outer * outer * outer)
            top = strength.astype(BF16)
            to[0][i, u:u + CHUNK] = top
            to[1][i, u:u + CHUNK] = (strength - top.astype(F32)).astype(BF16)


def gather_force(cols, acc, tile, span, of):
    part = cols[:, pl.ds(pl.multiple_of(span * ROWS, ROWS), ROWS)]
    top, rest = (jnp.concatenate([buf[i] for i in range(PARTS)], axis=1) for buf in of)
    acc[tile] += (jnp.dot(part, top, preferred_element_type=F32)
                  + jnp.dot(part, rest, preferred_element_type=F32))


def slot_index(dims, rep):
    slot = 0
    for i in range(3):
        base = min(dims[i], 3)
        slot = slot * base + (rep[i] + base) % base
    return slot


def gather_kernel(dims, mid_ref, line_ref, burg_ref, live_ref, pair_ref, blocks, ctrl, table, held, acc,
                  weights, basis, sums, live, pair, feat, tall, rows, cols, high0, low0, high1, low1,
                  load_sem, send_sem, recv_sem, part_send, part_recv, table_send, table_recv):
    me = tuple(lax.axis_index(a) for a in AXES)
    seg = live_ref.shape[1]
    kdims = tuple(d // 2 for d in dims)
    kcount = kdims[0] * kdims[1] * kdims[2]
    my_coarse = cell_id(tuple(me[i] // 2 for i in range(3)), kdims)
    loads = [pltpu.make_async_copy(src, dst, load_sem.at[k]) for k, (src, dst) in enumerate((
        (live_ref, live), (line_ref, blocks.at[0, :, pl.ds(3 * seg, 3 * seg)]),
        (mid_ref, blocks.at[0, :, pl.ds(0, 3 * seg)]),
        (burg_ref, blocks.at[0, :, pl.ds(6 * seg, 3 * seg)]), (pair_ref, pair)))]
    for load in loads:
        load.start()
    barrier = pltpu.get_barrier_semaphore()
    mesh_id = pl.DeviceIdType.MESH

    def at(rep):
        return tuple((me[i] - rep[i] + dims[i]) % dims[i] for i in range(3))

    def peer(step):
        other = (my_coarse + step) % kcount
        coarse = (other // (kdims[1] * kdims[2]), other // kdims[2] % kdims[1], other % kdims[2])
        return tuple(2 * coarse[i] + me[i] % 2 for i in range(3))

    steps = [tuple(r if i == axis else 0 for i in range(3))
             for axis in range(3) for r in reps(dims[axis]) if r != 0]
    for rep in steps:
        pl.semaphore_signal(barrier, inc=1, device_id=at(rep), device_id_type=mesh_id)

    def greet(step, carry):
        pl.semaphore_signal(barrier, inc=1, device_id=peer(step), device_id_type=mesh_id)
        return carry

    lax.fori_loop(1, kcount, greet, 0)

    held[...] = jnp.zeros_like(held)
    acc[...] = jnp.zeros_like(acc)
    for buf in (basis, weights, feat, tall, high1, low1):
        buf[...] = jnp.zeros_like(buf)
    for load in loads:
        load.wait()

    def row(c):
        return blocks[0, :, c * seg:(c + 1) * seg]

    alive = live[...].astype(F32)
    for c in range(3, 6):
        blocks[0, :, c * seg:(c + 1) * seg] = row(c) * alive
    lane = lax.broadcasted_iota(jnp.int32, (1, 128), 1)
    blocks[0, :, 9 * seg:9 * seg + 128] = jnp.where(lane == 13, jnp.sum(alive, axis=1, keepdims=True), 0.0)
    blocks[0, :, 9 * seg:9 * seg + 13] = pair[...].astype(F32)

    pl.semaphore_wait(barrier, len(steps) + kcount - 1)

    copies = {}

    def send(rep, axis):
        kept = tuple(0 if i == axis else rep[i] for i in range(3))
        moved = tuple(rep[i] if i == axis else 0 for i in range(3))
        slot = slot_index(dims, rep)
        copy = pltpu.make_async_remote_copy(
            src_ref=blocks.at[slot_index(dims, kept)], dst_ref=blocks.at[slot],
            send_sem=send_sem.at[slot], recv_sem=recv_sem.at[slot],
            device_id=at(moved), device_id_type=mesh_id)
        copy.start()
        copies[slot] = copy

    def arrived(rep):
        copies[slot_index(dims, rep)].wait_recv()

    xs, ys, zs = (reps(d)[1:] for d in dims)
    for r in zs:
        send((0, 0, r), 2)
    for r in xs:
        send((r, 0, 0), 0)
    for r in ys:
        send((0, r, 0), 1)

    z = [row(c) + ((me[c] % 2) - 1).astype(F32) for c in range(3)]
    terms = [jnp.ones_like(z[0])] + z + [z[a] * z[b] for a in range(3) for b in range(3)]
    for q in range(13):
        basis[q:q + 1] = terms[q]
    for a in range(3):
        for b in range(3):
            weights[3 * a + b:3 * a + b + 1] = row(6 + a) * row(3 + b)
    moments = lax.dot_general(weights[...], basis[...], NT, precision=lax.Precision.HIGHEST,
                              preferred_element_type=F32)
    sub = lax.broadcasted_iota(jnp.int32, moments.shape, 0)
    flat = jnp.where(sub == 0, moments, 0.0)
    for c in range(1, 9):
        flat = flat + pltpu.roll(jnp.where(sub == c, moments, 0.0), 13 * c, 1)
    sums[0] = jnp.sum(flat, axis=0, keepdims=True)

    def part_copy(axis):
        partner = tuple(me[i] + 1 - 2 * (me[i] % 2) if i == axis else me[i] for i in range(3))
        return pltpu.make_async_remote_copy(
            src_ref=sums.at[axis], dst_ref=sums.at[4 + axis], send_sem=part_send.at[axis],
            recv_sem=part_recv.at[axis], device_id=partner, device_id_type=mesh_id)

    def finish_part(axis):
        part_copy(axis).wait_recv()
        sums[axis + 1] = sums[axis] + sums[4 + axis]

    part_copy(0).start()
    for r in zs:
        arrived((0, 0, r))
        for a in xs:
            send((a, 0, r), 0)
        for b in ys:
            send((0, b, r), 1)
    for a in xs:
        arrived((a, 0, 0))
        for b in ys:
            send((a, b, 0), 1)
    finish_part(0)
    part_copy(1).start()
    for r in zs:
        for a in xs:
            arrived((a, 0, r))
            for b in ys:
                send((a, b, r), 1)
    finish_part(1)
    part_copy(2).start()
    finish_part(2)
    table[my_coarse] = sums[3]

    def table_copy(step):
        return pltpu.make_async_remote_copy(
            src_ref=table.at[my_coarse], dst_ref=table.at[my_coarse], send_sem=table_send.at[step],
            recv_sem=table_recv.at[step], device_id=peer(step), device_id_type=mesh_id)

    def start_table(step, carry):
        table_copy(step).start()
        return carry

    lax.fori_loop(1, kcount, start_table, 0)
    x = [row(c) - 0.5 for c in range(3)]
    hold_targets(row, x, feat, weights, held)
    rows[...], cols[...] = lay_sources(row, x, feat, weights, tall)
    spans = seg // ROWS
    buffers = ((high0, low0), (high1, low1))

    def own_tile(tile, carry):
        for k in range(spans):
            strengths(held, rows, tile, k, buffers[k % 2])
            before = jnp.maximum(tile * spans + k - 1, 0)
            gather_force(cols, acc, before // spans, before % spans, buffers[1 - k % 2])
        return carry

    lax.fori_loop(0, seg // LANES, own_tile, 0)
    gather_force(cols, acc, seg // LANES - 1, spans - 1, buffers[1])
    for rep in [(a, b, r) for r in [0] + zs for a in [0] + xs for b in ys]:
        arrived(rep)

    def wait_table(step, carry):
        table_copy(step).wait()
        return carry

    lax.fori_loop(1, kcount, wait_table, 0)
    for axis in range(3):
        part_copy(axis).wait_send()
    for copy in copies.values():
        copy.wait_send()
    for slot in range(blocks.shape[0]):
        ctrl[slot] = blocks[slot, :, 9 * seg:9 * seg + 128]


def force_kernel(dims, scalars, table, blocks, held, own, out,
                 feat, wide, tall, rows, cols, high0, low0, high1, low1, acc, eight):
    me = tuple(lax.axis_index(a) for a in AXES)
    tiles = held.shape[0] - 1
    seg = tiles * LANES
    width = seg // 8
    kdims = tuple(d // 2 for d in dims)
    kcount = kdims[0] * kdims[1] * kdims[2]
    for buf in (feat, wide, tall, high1, low1):
        buf[...] = jnp.zeros_like(buf)
    acc[...] = own[...]
    for c in range(9):
        for s in range(8):
            eight[c, s:s + 1] = blocks[0, :, c * seg + s * width:c * seg + (s + 1) * width]

    def append_source(t, at):
        offset = (t // 9 - 1, t // 3 % 3 - 1, t % 3 - 1)
        slot = slot_index(dims, offset)
        ahead = t > 13
        flag = scalars[jnp.where(ahead, 0, slot), 0,
                       jnp.where(ahead, t - 14, jnp.maximum(12 - t, 0))]
        listed = jnp.logical_and(t != 13, flag > 0.0)

        @pl.when(listed)
        def _():
            def row(c):
                return blocks[slot, :, c * seg:(c + 1) * seg]

            y = [row(c) + (offset[c].astype(F32) - 0.5) for c in range(3)]
            here = pl.ds(pl.multiple_of(at, GRAIN), seg)
            rows[here, :], cols[:, here] = lay_sources(row, y, feat, wide, tall)

        size = (scalars[slot, 0, 13].astype(jnp.int32) + (GRAIN - 1)) // GRAIN * GRAIN
        return at + jnp.where(listed, size, 0)

    total = lax.fori_loop(0, 27, append_source, 0)
    lane = lax.broadcasted_iota(jnp.int32, (ROWS, 128), 1)
    rows[pl.ds(pl.multiple_of(total, GRAIN), ROWS), :] = (lane == 3).astype(F32).astype(BF16)
    cols[:, pl.ds(pl.multiple_of(total, GRAIN), ROWS)] = jnp.zeros((16, ROWS), BF16)

    my_tiles = (scalars[0, 0, 13].astype(jnp.int32) + (LANES - 1)) // LANES
    spans = (total + (ROWS - 1)) // ROWS
    steps = my_tiles * spans
    buffers = ((high0, low0), (high1, low1))

    def place(step):
        done = step >= steps
        tile = jnp.where(done, tiles, step // spans)
        return tile, jnp.where(done, 0, step % spans)

    def some_steps(first, many):
        for k in range(many):
            strengths(held, rows, *place(first + k), buffers[k % 2])
            gather_force(cols, acc, *place(jnp.maximum(first + k - 1, 0)), buffers[1 - k % 2])

    def many_steps(i, carry):
        some_steps(i * UNROLL, UNROLL)
        return carry

    def two_steps(i, carry):
        some_steps(i * 2, 2)
        return carry

    groups = steps // UNROLL
    pairs = (steps + 1) // 2
    lax.fori_loop(0, groups, many_steps, 0)
    lax.fori_loop(groups * (UNROLL // 2), pairs, two_steps, 0)

    @pl.when(pairs > 0)
    def _():
        gather_force(cols, acc, *place(pairs * 2 - 1), buffers[1])


    slot_id = lax.broadcasted_iota(jnp.int32, (8, width), 0) * width + lax.broadcasted_iota(
        jnp.int32, (8, width), 1)
    alive = (slot_id.astype(F32) < scalars[0, 0, 13]).astype(F32)
    w8 = [eight[6 + a] * eight[3 + b] for a in range(3) for b in range(3)]

    def far_step(k, grads):
        kc = (k // (kdims[1] * kdims[2]), k // kdims[2] % kdims[1], k % kdims[2])
        u = []
        for i in range(3):
            gap = (me[i] - 2 * kc[i] + dims[i] + dims[i] // 2) % dims[i] - dims[i] // 2
            u.append(eight[i] + (gap.astype(F32) - 1.0))
        q = []
        for m in range(13):
            value = table[k, 0, m] * w8[0]
            for c in range(1, 9):
                value = value + table[k, 0, 13 * c + m] * w8[c]
            q.append(value)
        inv = lax.rsqrt(u[0] * u[0] + u[1] * u[1] + u[2] * u[2] + SPLIT_SQ)
        inv2 = inv * inv
        inv3 = inv2 * inv
        inv5 = inv3 * inv2
        inv7 = inv5 * inv2
        dip = q[1] * u[0] + q[2] * u[1] + q[3] * u[2]
        quad = [q[4 + 3 * a] * u[0] + q[5 + 3 * a] * u[1] + q[6 + 3 * a] * u[2] for a in range(3)]
        form = quad[0] * u[0] + quad[1] * u[1] + quad[2] * u[2]
        trace = q[4] + q[8] + q[12]
        radial = (1.5 * trace - 3.0 * dip) * inv5 - q[0] * inv3 - 7.5 * form * inv7
        return tuple(grads[c] + u[c] * radial + q[1 + c] * inv3 + 3.0 * quad[c] * inv5
                     for c in range(3))

    zero = jnp.zeros((8, width), F32)
    grads = lax.fori_loop(0, kcount, far_step, (zero, zero, zero))
    for c in range(3):
        for t in range(tiles):
            turned = acc[t]
            near = (blocks[0, :, c * seg + t * LANES:c * seg + (t + 1) * LANES] - 0.5) * turned[4:5] - (turned[c:c + 1] + turned[8 + c:9 + c] + turned[12 + c:13 + c])
            for s in range(t * LANES // width, (t + 1) * LANES // width):
                inside = slice(s * width - t * LANES, (s + 1) * width - t * LANES)
                out[c, :, s * width:(s + 1) * width] = (near[:, inside] - grads[c][s:s + 1]) * alive[s:s + 1]


def on_device(dims, midpoints, line_vectors, burgers, live_mask, pair_list):
    seg = midpoints.shape[4]
    count = dims[0] * dims[1] * dims[2]
    kcount = count // 8
    slots = len(reps(dims[0])) * len(reps(dims[1])) * len(reps(dims[2]))
    vmem = pl.BlockSpec(memory_space=pltpu.VMEM)
    smem = pl.BlockSpec(memory_space=pltpu.SMEM)
    hbm = pl.BlockSpec(memory_space=pltpu.HBM)
    strength_buffer = pltpu.VMEM((PARTS, ROWS, 128), BF16)
    targets = (seg // LANES + 1, 2 * PARTS, 128, 128)
    sums = (seg // LANES + 1, 16, LANES)
    blocks, ctrl, table, held, own = pl.pallas_call(
        functools.partial(gather_kernel, dims),
        out_shape=(jax.ShapeDtypeStruct((slots, 1, 9 * seg + 128), F32),
                   jax.ShapeDtypeStruct((slots, 1, 128), F32),
                   jax.ShapeDtypeStruct((kcount, 1, 128), F32),
                   jax.ShapeDtypeStruct(targets, BF16),
                   jax.ShapeDtypeStruct(sums, F32)),
        in_specs=[hbm] * 5,
        out_specs=(vmem,) * 5,
        scratch_shapes=[
            pltpu.VMEM((16, seg), F32),
            pltpu.VMEM((128, seg), F32),
            pltpu.VMEM((7, 1, 128), F32),
            pltpu.VMEM((1, seg), jnp.int32),
            pltpu.VMEM((1, 13), jnp.int32),
            pltpu.VMEM((8, seg), F32),
            pltpu.VMEM((128, seg), F32),
            pltpu.VMEM((seg, 128), BF16),
            pltpu.VMEM((16, seg), BF16),
            *[strength_buffer] * 4,
            pltpu.SemaphoreType.DMA((5,)),
            pltpu.SemaphoreType.DMA((slots,)),
            pltpu.SemaphoreType.DMA((slots,)),
            pltpu.SemaphoreType.DMA((3,)),
            pltpu.SemaphoreType.DMA((3,)),
            pltpu.SemaphoreType.DMA((kcount,)),
            pltpu.SemaphoreType.DMA((kcount,)),
        ],
        compiler_params=pltpu.CompilerParams(collective_id=0, has_side_effects=True),
        name="gather",
    )(*(a.reshape(1, 3 * seg) for a in (midpoints, line_vectors, burgers)),
      live_mask.reshape(1, seg), pair_list.reshape(1, 13))
    out = pl.pallas_call(
        functools.partial(force_kernel, dims),
        out_shape=jax.ShapeDtypeStruct((3, 1, seg), F32),
        in_specs=[smem] * 2 + [vmem] * 3,
        out_specs=vmem,
        scratch_shapes=[
            pltpu.VMEM((8, seg), F32),
            pltpu.VMEM((16, seg), F32),
            pltpu.VMEM((128, seg), F32),
            pltpu.VMEM((27 * seg + ROWS, 128), BF16),
            pltpu.VMEM((16, 27 * seg + ROWS), BF16),
            *[strength_buffer] * 4,
            pltpu.VMEM(sums, F32),
            pltpu.VMEM((9, 8, seg // 8), F32),
        ],
        compiler_params=pltpu.CompilerParams(vmem_limit_bytes=60 * 2**20),
        name="forces",
    )(ctrl, table, blocks, held, own)
    return out.reshape(3, 1, 1, 1, seg)


def solution(mesh):
    dims = tuple(mesh.shape[a] for a in AXES)
    placed = (
        P(None, "gx", "gy", "gz", None),
        P(None, "gx", "gy", "gz", None),
        P(None, "gx", "gy", "gz", None),
        P("gx", "gy", "gz", None),
        P(None, "gx", "gy", "gz"),
    )
    return jax.shard_map(
        functools.partial(on_device, dims),
        mesh=mesh,
        in_specs=placed,
        out_specs=P(None, "gx", "gy", "gz", None),
        check_vma=False,
    )
```

```python
import functools

import jax
import jax.numpy as jnp
from jax import lax
from jax.experimental import pallas as pl
from jax.experimental.pallas import tpu as pltpu
from jax.sharding import PartitionSpec as P

AXES = ("gx", "gy", "gz")
CORE_SQ = 0.1 * 0.1
SPLIT_SQ = 2.0 * 2.0
LANES = 256
ROWS = 512
CHUNK = 256
UNROLL = 8
PARTS = LANES // 128
GRAIN = 128
F32 = jnp.float32
BF16 = jnp.bfloat16
NT = (((1,), (1,)), ((), ()))


def reps(size):
    return [0] if size == 1 else [0, 1] if size == 2 else [0, 1, -1]


def cell_id(cell, dims):
    return (cell[0] * dims[1] + cell[1]) * dims[2] + cell[2]


def split3(value):
    high = value.astype(BF16).astype(F32)
    rest = value - high
    middle = rest.astype(BF16).astype(F32)
    return high, middle, rest - middle


def split_coupling(row, wide):
    for a in range(3):
        for b in range(3):
            wide[3 * a + b:3 * a + b + 1] = row(6 + a) * row(3 + b)
    whole = wide[...]
    high = whole.astype(BF16).astype(F32)
    return high, whole - high


def hold_targets(row, x, feat, wide, held):
    for c in range(3):
        feat[c:c + 1] = -2.0 * x[c]
    feat[3:4] = jnp.ones_like(x[0])
    feat[4:5] = x[0] * x[0] + x[1] * x[1] + x[2] * x[2] + CORE_SQ
    high, middle, low = split3(feat[...])
    whigh, wlow = split_coupling(row, wide)
    distance = jnp.concatenate([high, high, high, middle, middle, low], axis=0).astype(BF16)
    coupling = jnp.concatenate([whigh, whigh, wlow], axis=0).astype(BF16)
    for t in range(held.shape[0] - 1):
        for i in range(PARTS):
            cut = slice(t * LANES + i * 128, t * LANES + (i + 1) * 128)
            held[t, i, 0:48] = distance[:, cut]
            held[t, PARTS + i, 48:96] = coupling[:, cut]


def lay_sources(row, y, feat, wide, tall):
    for c in range(3):
        feat[c:c + 1] = y[c]
    feat[3:4] = y[0] * y[0] + y[1] * y[1] + y[2] * y[2]
    feat[4:5] = jnp.ones_like(y[0])
    high, middle, low = split3(feat[...])
    for k, part in enumerate((high, middle, low, high, middle, high)):
        tall[8 * k:8 * k + 8] = part
    whigh, wlow = split_coupling(row, wide)
    tall[48:64] = whigh
    tall[64:80] = wlow
    tall[80:96] = whigh
    return (jnp.transpose(tall[...].astype(BF16)),
            jnp.concatenate([high, middle + pltpu.roll(low, 4, 0)], axis=0).astype(BF16))


def strengths(held, rows, tile, span, to):
    w = jnp.concatenate([held[tile, i] for i in range(2 * PARTS)], axis=1)
    for u in range(0, ROWS, CHUNK):
        lhs = rows[pl.ds(pl.multiple_of(span * ROWS + u, CHUNK), CHUNK), :]
        product = jnp.dot(lhs, w, preferred_element_type=F32)
        for i in range(PARTS):
            near = product[:, i * 128:(i + 1) * 128]
            pull = product[:, LANES + i * 128:LANES + (i + 1) * 128]
            inner = lax.rsqrt(near)
            outer = lax.rsqrt(near + (SPLIT_SQ - CORE_SQ))
            strength = pull * (inner * inner * inner - outer * outer * outer)
            top = strength.astype(BF16)
            to[0][i, u:u + CHUNK] = top
            to[1][i, u:u + CHUNK] = (strength - top.astype(F32)).astype(BF16)


def gather_force(cols, acc, tile, span, of):
    part = cols[:, pl.ds(pl.multiple_of(span * ROWS, ROWS), ROWS)]
    top, rest = (jnp.concatenate([buf[i] for i in range(PARTS)], axis=1) for buf in of)
    acc[tile] += (jnp.dot(part, top, preferred_element_type=F32)
                  + jnp.dot(part, rest, preferred_element_type=F32))


def slot_index(dims, rep):
    slot = 0
    for i in range(3):
        base = min(dims[i], 3)
        slot = slot * base + (rep[i] + base) % base
    return slot


def gather_kernel(dims, mid_ref, line_ref, burg_ref, live_ref, pair_ref, blocks, ctrl, table, held, acc,
                  weights, basis, sums, live, pair, feat, tall, rows, cols, high0, low0, high1, low1,
                  load_sem, send_sem, recv_sem, part_send, part_recv, table_send, table_recv):
    me = tuple(lax.axis_index(a) for a in AXES)
    seg = live_ref.shape[1]
    kdims = tuple(d // 2 for d in dims)
    kcount = kdims[0] * kdims[1] * kdims[2]
    my_coarse = cell_id(tuple(me[i] // 2 for i in range(3)), kdims)
    loads = [pltpu.make_async_copy(src, dst, load_sem.at[k]) for k, (src, dst) in enumerate((
        (live_ref, live), (line_ref, blocks.at[0, :, pl.ds(3 * seg, 3 * seg)]),
        (mid_ref, blocks.at[0, :, pl.ds(0, 3 * seg)]),
        (burg_ref, blocks.at[0, :, pl.ds(6 * seg, 3 * seg)]), (pair_ref, pair)))]
    for load in loads:
        load.start()
    barrier = pltpu.get_barrier_semaphore()
    mesh_id = pl.DeviceIdType.MESH

    def at(rep):
        return tuple((me[i] - rep[i] + dims[i]) % dims[i] for i in range(3))

    def peer(step):
        other = (my_coarse + step) % kcount
        coarse = (other // (kdims[1] * kdims[2]), other // kdims[2] % kdims[1], other % kdims[2])
        return tuple(2 * coarse[i] + me[i] % 2 for i in range(3))

    steps = [tuple(r if i == axis else 0 for i in range(3))
             for axis in range(3) for r in reps(dims[axis]) if r != 0]
    parity = tuple(me[i] % 2 for i in range(3))
    my_part = parity[0] * 4 + parity[1] * 2 + parity[2]

    def partner(step):
        bits = (step // 4, step // 2 % 2, step % 2)
        return tuple(me[i] + bits[i] * (1 - 2 * parity[i]) for i in range(3))

    diagonal = (3, 5, 6, 7)
    for rep in steps:
        pl.semaphore_signal(barrier, inc=1, device_id=at(rep), device_id_type=mesh_id)
    for step in diagonal:
        pl.semaphore_signal(barrier, inc=1, device_id=partner(step), device_id_type=mesh_id)

    def greet(step, carry):
        pl.semaphore_signal(barrier, inc=1, device_id=peer(step), device_id_type=mesh_id)
        return carry

    lax.fori_loop(1, kcount, greet, 0)

    held[...] = jnp.zeros_like(held)
    acc[...] = jnp.zeros_like(acc)
    for buf in (basis, weights, feat, tall, high1, low1):
        buf[...] = jnp.zeros_like(buf)
    for load in loads:
        load.wait()

    def row(c):
        return blocks[0, :, c * seg:(c + 1) * seg]

    alive = live[...].astype(F32)
    for c in range(3, 6):
        blocks[0, :, c * seg:(c + 1) * seg] = row(c) * alive
    lane = lax.broadcasted_iota(jnp.int32, (1, 128), 1)
    blocks[0, :, 9 * seg:9 * seg + 128] = jnp.where(lane == 13, jnp.sum(alive, axis=1, keepdims=True), 0.0)
    blocks[0, :, 9 * seg:9 * seg + 13] = pair[...].astype(F32)

    z = [row(c) + ((me[c] % 2) - 1).astype(F32) for c in range(3)]
    terms = [jnp.ones_like(z[0])] + z + [z[a] * z[b] for a in range(3) for b in range(3)]
    for q in range(13):
        basis[q:q + 1] = terms[q]
    for a in range(3):
        for b in range(3):
            weights[3 * a + b:3 * a + b + 1] = row(6 + a) * row(3 + b)
    moments = lax.dot_general(weights[...], basis[...], NT, precision=lax.Precision.HIGHEST,
                              preferred_element_type=F32)
    sub = lax.broadcasted_iota(jnp.int32, moments.shape, 0)
    flat = jnp.where(sub == 0, moments, 0.0)
    for c in range(1, 9):
        flat = flat + pltpu.roll(jnp.where(sub == c, moments, 0.0), 13 * c, 1)
    sums[my_part] = jnp.sum(flat, axis=0, keepdims=True)

    pl.semaphore_wait(barrier, len(steps) + len(diagonal) + kcount - 1)

    def part_copy(step):
        return pltpu.make_async_remote_copy(
            src_ref=sums.at[my_part], dst_ref=sums.at[my_part], send_sem=part_send.at[step],
            recv_sem=part_recv.at[step], device_id=partner(step), device_id_type=mesh_id)

    for step in range(1, 8):
        part_copy(step).start()

    copies = {}

    def send(rep, axis):
        kept = tuple(0 if i == axis else rep[i] for i in range(3))
        moved = tuple(rep[i] if i == axis else 0 for i in range(3))
        slot = slot_index(dims, rep)
        copy = pltpu.make_async_remote_copy(
            src_ref=blocks.at[slot_index(dims, kept)], dst_ref=blocks.at[slot],
            send_sem=send_sem.at[slot], recv_sem=recv_sem.at[slot],
            device_id=at(moved), device_id_type=mesh_id)
        copy.start()
        copies[slot] = copy

    waited = set()

    def arrived(rep):
        if rep not in waited:
            waited.add(rep)
            copies[slot_index(dims, rep)].wait_recv()

    xs, ys, zs = (reps(d)[1:] for d in dims)
    for r in zs:
        send((0, 0, r), 2)
    for r in xs:
        send((r, 0, 0), 0)
    for r in ys:
        send((0, r, 0), 1)

    for r in zs:
        arrived((0, 0, r))
        for a in xs:
            send((a, 0, r), 0)
        for b in ys:
            send((0, b, r), 1)
    for b in ys:
        arrived((0, b, 0))
        for a in xs:
            send((a, b, 0), 0)
    for step in range(1, 8):
        part_copy(step).wait_recv()
    total = sums[0]
    for k in range(1, 8):
        total = total + sums[k]
    table[my_coarse] = total

    def table_copy(step):
        return pltpu.make_async_remote_copy(
            src_ref=table.at[my_coarse], dst_ref=table.at[my_coarse], send_sem=table_send.at[step],
            recv_sem=table_recv.at[step], device_id=peer(step), device_id_type=mesh_id)

    def start_table(step, carry):
        table_copy(step).start()
        return carry

    lax.fori_loop(1, kcount, start_table, 0)

    x = [row(c) - 0.5 for c in range(3)]
    hold_targets(row, x, feat, weights, held)
    rows[...], cols[...] = lay_sources(row, x, feat, weights, tall)
    for r in zs:
        for a in xs:
            arrived((a, 0, r))
            for b in ys:
                send((a, b, r), 1)
    spans = seg // ROWS
    tiles = seg // LANES
    buffers = ((high0, low0), (high1, low1))

    def own_tile(tile, carry):
        for k in range(spans):
            strengths(held, rows, tile, k, buffers[k % 2])
            before = jnp.maximum(tile * spans + k - 1, 0)
            gather_force(cols, acc, before // spans, before % spans, buffers[1 - k % 2])
        return carry

    lax.fori_loop(0, tiles, own_tile, 0)
    gather_force(cols, acc, tiles - 1, spans - 1, buffers[1])
    for rep in [(a, b, r) for r in [0] + zs for a in [0] + xs for b in [0] + ys]:
        if rep != (0, 0, 0):
            arrived(rep)

    def wait_table(step, carry):
        table_copy(step).wait()
        return carry

    lax.fori_loop(1, kcount, wait_table, 0)
    for step in range(1, 8):
        part_copy(step).wait_send()
    for copy in copies.values():
        copy.wait_send()
    for slot in range(blocks.shape[0]):
        ctrl[slot] = blocks[slot, :, 9 * seg:9 * seg + 128]


def force_kernel(dims, scalars, table, blocks, held, own, out,
                 feat, wide, tall, rows, cols, high0, low0, high1, low1, acc, eight, todo):
    me = tuple(lax.axis_index(a) for a in AXES)
    tiles = held.shape[0] - 1
    seg = tiles * LANES
    width = seg // 8
    kdims = tuple(d // 2 for d in dims)
    kcount = kdims[0] * kdims[1] * kdims[2]
    for buf in (feat, wide, tall, high1, low1):
        buf[...] = jnp.zeros_like(buf)
    acc[...] = own[...]
    for c in range(9):
        for s in range(8):
            eight[c, s:s + 1] = blocks[0, :, c * seg + s * width:c * seg + (s + 1) * width]

    def list_source(t, carry):
        at, found = carry
        slot = slot_index(dims, (t // 9 - 1, t // 3 % 3 - 1, t % 3 - 1))
        ahead = t > 13
        flag = scalars[jnp.where(ahead, 0, slot), 0,
                       jnp.where(ahead, t - 14, jnp.maximum(12 - t, 0))]
        listed = jnp.logical_and(t != 13, flag > 0.0)
        todo[0, found] = t
        todo[1, found] = at
        size = (scalars[slot, 0, 13].astype(jnp.int32) + (GRAIN - 1)) // GRAIN * GRAIN
        return at + jnp.where(listed, size, 0), found + listed.astype(jnp.int32)

    total, found = lax.fori_loop(0, 27, list_source, (0, 0))
    todo[0, found] = 13
    todo[1, found] = total

    def two_sources(i, carry):
        laid = []
        for k in range(2):
            t, at = todo[0, 2 * i + k], todo[1, 2 * i + k]
            offset = (t // 9 - 1, t // 3 % 3 - 1, t % 3 - 1)
            slot = slot_index(dims, offset)

            def row(c, slot=slot):
                return blocks[slot, :, c * seg:(c + 1) * seg]

            y = [row(c) + (offset[c].astype(F32) - 0.5) for c in range(3)]
            laid.append((at, lay_sources(row, y, feat.at[k], wide.at[k], tall.at[k])))
        for at, (row_part, col_part) in laid:
            here = pl.ds(pl.multiple_of(at, GRAIN), seg)
            rows[here, :] = row_part
            cols[:, here] = col_part
        return carry

    lax.fori_loop(0, (found + 1) // 2, two_sources, 0)
    lane = lax.broadcasted_iota(jnp.int32, (ROWS, 128), 1)
    rows[pl.ds(pl.multiple_of(total, GRAIN), ROWS), :] = (lane == 3).astype(F32).astype(BF16)
    cols[:, pl.ds(pl.multiple_of(total, GRAIN), ROWS)] = jnp.zeros((16, ROWS), BF16)

    my_tiles = (scalars[0, 0, 13].astype(jnp.int32) + (LANES - 1)) // LANES
    spans = (total + (ROWS - 1)) // ROWS
    steps = my_tiles * spans
    buffers = ((high0, low0), (high1, low1))

    def place(step):
        done = step >= steps
        tile = jnp.where(done, tiles, step // spans)
        return tile, jnp.where(done, 0, step % spans)

    def some_steps(first, many):
        for k in range(many):
            strengths(held, rows, *place(first + k), buffers[k % 2])
            gather_force(cols, acc, *place(jnp.maximum(first + k - 1, 0)), buffers[1 - k % 2])

    def many_steps(i, carry):
        some_steps(i * UNROLL, UNROLL)
        return carry

    def two_steps(i, carry):
        some_steps(i * 2, 2)
        return carry

    groups = steps // UNROLL
    pairs = (steps + 1) // 2
    lax.fori_loop(0, groups, many_steps, 0)
    lax.fori_loop(groups * (UNROLL // 2), pairs, two_steps, 0)

    @pl.when(pairs > 0)
    def _():
        gather_force(cols, acc, *place(pairs * 2 - 1), buffers[1])


    slot_id = lax.broadcasted_iota(jnp.int32, (8, width), 0) * width + lax.broadcasted_iota(
        jnp.int32, (8, width), 1)
    alive = (slot_id.astype(F32) < scalars[0, 0, 13]).astype(F32)
    w8 = [eight[6 + a] * eight[3 + b] for a in range(3) for b in range(3)]

    def far_step(k, grads):
        kc = (k // (kdims[1] * kdims[2]), k // kdims[2] % kdims[1], k % kdims[2])
        u = []
        for i in range(3):
            gap = (me[i] - 2 * kc[i] + dims[i] + dims[i] // 2) % dims[i] - dims[i] // 2
            u.append(eight[i] + (gap.astype(F32) - 1.0))
        q = []
        for m in range(13):
            value = table[k, 0, m] * w8[0]
            for c in range(1, 9):
                value = value + table[k, 0, 13 * c + m] * w8[c]
            q.append(value)
        inv = lax.rsqrt(u[0] * u[0] + u[1] * u[1] + u[2] * u[2] + SPLIT_SQ)
        inv2 = inv * inv
        inv3 = inv2 * inv
        inv5 = inv3 * inv2
        inv7 = inv5 * inv2
        dip = q[1] * u[0] + q[2] * u[1] + q[3] * u[2]
        quad = [q[4 + 3 * a] * u[0] + q[5 + 3 * a] * u[1] + q[6 + 3 * a] * u[2] for a in range(3)]
        form = quad[0] * u[0] + quad[1] * u[1] + quad[2] * u[2]
        trace = q[4] + q[8] + q[12]
        radial = (1.5 * trace - 3.0 * dip) * inv5 - q[0] * inv3 - 7.5 * form * inv7
        return tuple(grads[c] + u[c] * radial + q[1 + c] * inv3 + 3.0 * quad[c] * inv5
                     for c in range(3))

    zero = jnp.zeros((8, width), F32)
    grads = lax.fori_loop(0, kcount, far_step, (zero, zero, zero))
    for c in range(3):
        for t in range(tiles):
            turned = acc[t]
            near = (blocks[0, :, c * seg + t * LANES:c * seg + (t + 1) * LANES] - 0.5) * turned[4:5] - (turned[c:c + 1] + turned[8 + c:9 + c] + turned[12 + c:13 + c])
            for s in range(t * LANES // width, (t + 1) * LANES // width):
                inside = slice(s * width - t * LANES, (s + 1) * width - t * LANES)
                out[c, :, s * width:(s + 1) * width] = (near[:, inside] - grads[c][s:s + 1]) * alive[s:s + 1]


def on_device(dims, midpoints, line_vectors, burgers, live_mask, pair_list):
    seg = midpoints.shape[4]
    count = dims[0] * dims[1] * dims[2]
    kcount = count // 8
    slots = len(reps(dims[0])) * len(reps(dims[1])) * len(reps(dims[2]))
    vmem = pl.BlockSpec(memory_space=pltpu.VMEM)
    smem = pl.BlockSpec(memory_space=pltpu.SMEM)
    hbm = pl.BlockSpec(memory_space=pltpu.HBM)
    strength_buffer = pltpu.VMEM((PARTS, ROWS, 128), BF16)
    targets = (seg // LANES + 1, 2 * PARTS, 128, 128)
    sums = (seg // LANES + 1, 16, LANES)
    blocks, ctrl, table, held, own = pl.pallas_call(
        functools.partial(gather_kernel, dims),
        out_shape=(jax.ShapeDtypeStruct((slots, 1, 9 * seg + 128), F32),
                   jax.ShapeDtypeStruct((slots, 1, 128), F32),
                   jax.ShapeDtypeStruct((kcount, 1, 128), F32),
                   jax.ShapeDtypeStruct(targets, BF16),
                   jax.ShapeDtypeStruct(sums, F32)),
        in_specs=[hbm] * 5,
        out_specs=(vmem,) * 5,
        scratch_shapes=[
            pltpu.VMEM((16, seg), F32),
            pltpu.VMEM((128, seg), F32),
            pltpu.VMEM((8, 1, 128), F32),
            pltpu.VMEM((1, seg), jnp.int32),
            pltpu.VMEM((1, 13), jnp.int32),
            pltpu.VMEM((8, seg), F32),
            pltpu.VMEM((128, seg), F32),
            pltpu.VMEM((seg, 128), BF16),
            pltpu.VMEM((16, seg), BF16),
            *[strength_buffer] * 4,
            pltpu.SemaphoreType.DMA((5,)),
            pltpu.SemaphoreType.DMA((slots,)),
            pltpu.SemaphoreType.DMA((slots,)),
            pltpu.SemaphoreType.DMA((8,)),
            pltpu.SemaphoreType.DMA((8,)),
            pltpu.SemaphoreType.DMA((kcount,)),
            pltpu.SemaphoreType.DMA((kcount,)),
        ],
        compiler_params=pltpu.CompilerParams(collective_id=0, has_side_effects=True),
        name="gather",
    )(*(a.reshape(1, 3 * seg) for a in (midpoints, line_vectors, burgers)),
      live_mask.reshape(1, seg), pair_list.reshape(1, 13))
    out = pl.pallas_call(
        functools.partial(force_kernel, dims),
        out_shape=jax.ShapeDtypeStruct((3, 1, seg), F32),
        in_specs=[smem] * 2 + [vmem] * 3,
        out_specs=vmem,
        scratch_shapes=[
            pltpu.VMEM((2, 8, seg), F32),
            pltpu.VMEM((2, 16, seg), F32),
            pltpu.VMEM((2, 128, seg), F32),
            pltpu.VMEM((27 * seg + ROWS, 128), BF16),
            pltpu.VMEM((16, 27 * seg + ROWS), BF16),
            *[strength_buffer] * 4,
            pltpu.VMEM(sums, F32),
            pltpu.VMEM((9, 8, seg // 8), F32),
            pltpu.SMEM((2, 32), jnp.int32),
        ],
        compiler_params=pltpu.CompilerParams(vmem_limit_bytes=60 * 2**20),
        name="forces",
    )(ctrl, table, blocks, held, own)
    return out.reshape(3, 1, 1, 1, seg)


def solution(mesh):
    dims = tuple(mesh.shape[a] for a in AXES)
    placed = (
        P(None, "gx", "gy", "gz", None),
        P(None, "gx", "gy", "gz", None),
        P(None, "gx", "gy", "gz", None),
        P("gx", "gy", "gz", None),
        P(None, "gx", "gy", "gz"),
    )
    return jax.shard_map(
        functools.partial(on_device, dims),
        mesh=mesh,
        in_specs=placed,
        out_specs=P(None, "gx", "gy", "gz", None),
        check_vma=False,
    )
```

```python
import functools

import jax
import jax.numpy as jnp
from jax import lax
from jax.experimental import pallas as pl
from jax.experimental.pallas import tpu as pltpu
from jax.sharding import PartitionSpec as P

AXES = ("gx", "gy", "gz")
CORE_SQ = 0.1 * 0.1
SPLIT_SQ = 2.0 * 2.0
LANES = 256
ROWS = 512
CHUNK = 256
UNROLL = 12
PARTS = LANES // 128
GRAIN = 128
F32 = jnp.float32
BF16 = jnp.bfloat16
NT = (((1,), (1,)), ((), ()))


def reps(size):
    return [0] if size == 1 else [0, 1] if size == 2 else [0, 1, -1]


def cell_id(cell, dims):
    return (cell[0] * dims[1] + cell[1]) * dims[2] + cell[2]


def split3(value):
    high = value.astype(BF16).astype(F32)
    rest = value - high
    middle = rest.astype(BF16).astype(F32)
    return high, middle, rest - middle


def split_coupling(row, wide):
    for a in range(3):
        for b in range(3):
            wide[3 * a + b:3 * a + b + 1] = row(6 + a) * row(3 + b)
    whole = wide[...]
    high = whole.astype(BF16).astype(F32)
    return high, whole - high


def hold_targets(row, x, feat, wide, held):
    for c in range(3):
        feat[c:c + 1] = -2.0 * x[c]
    feat[3:4] = jnp.ones_like(x[0])
    feat[4:5] = x[0] * x[0] + x[1] * x[1] + x[2] * x[2] + CORE_SQ
    high, middle, low = split3(feat[...])
    whigh, wlow = split_coupling(row, wide)
    distance = jnp.concatenate([high, high, high, middle, middle, low], axis=0).astype(BF16)
    coupling = jnp.concatenate([whigh, whigh, wlow], axis=0).astype(BF16)
    for t in range(held.shape[0] - 1):
        for i in range(PARTS):
            cut = slice(t * LANES + i * 128, t * LANES + (i + 1) * 128)
            held[t, i, 0:48] = distance[:, cut]
            held[t, PARTS + i, 48:96] = coupling[:, cut]


def lay_sources(row, y, feat, wide, tall):
    for c in range(3):
        feat[c:c + 1] = y[c]
    feat[3:4] = y[0] * y[0] + y[1] * y[1] + y[2] * y[2]
    feat[4:5] = jnp.ones_like(y[0])
    high, middle, low = split3(feat[...])
    for k, part in enumerate((high, middle, low, high, middle, high)):
        tall[8 * k:8 * k + 8] = part
    whigh, wlow = split_coupling(row, wide)
    tall[48:64] = whigh
    tall[64:80] = wlow
    tall[80:96] = whigh
    return (jnp.transpose(tall[...].astype(BF16)),
            jnp.concatenate([high, middle + pltpu.roll(low, 4, 0)], axis=0).astype(BF16))


def strengths(held, rows, tile, span, to):
    w = jnp.concatenate([held[tile, i] for i in range(2 * PARTS)], axis=1)
    for u in range(0, ROWS, CHUNK):
        lhs = rows[pl.ds(pl.multiple_of(span * ROWS + u, CHUNK), CHUNK), :]
        product = jnp.dot(lhs, w, preferred_element_type=F32)
        for i in range(PARTS):
            near = product[:, i * 128:(i + 1) * 128]
            pull = product[:, LANES + i * 128:LANES + (i + 1) * 128]
            inner = lax.rsqrt(near)
            outer = lax.rsqrt(near + (SPLIT_SQ - CORE_SQ))
            strength = pull * (inner * inner * inner - outer * outer * outer)
            top = strength.astype(BF16)
            to[0][i, u:u + CHUNK] = top
            to[1][i, u:u + CHUNK] = (strength - top.astype(F32)).astype(BF16)


def gather_force(cols, acc, tile, span, of):
    part = cols[:, pl.ds(pl.multiple_of(span * ROWS, ROWS), ROWS)]
    top, rest = (jnp.concatenate([buf[i] for i in range(PARTS)], axis=1) for buf in of)
    acc[tile] += (jnp.dot(part, top, preferred_element_type=F32)
                  + jnp.dot(part, rest, preferred_element_type=F32))


def slot_index(dims, rep):
    slot = 0
    for i in range(3):
        base = min(dims[i], 3)
        slot = slot * base + (rep[i] + base) % base
    return slot


def gather_kernel(dims, mid_ref, line_ref, burg_ref, live_ref, pair_ref, blocks, ctrl, held, acc, far,
                  weights, basis, sums, table, table_s, eight, live, pair, feat, tall, rows, cols, high0, low0, high1, low1,
                  load_sem, send_sem, recv_sem, part_send, part_recv, table_send, table_recv):
    me = tuple(lax.axis_index(a) for a in AXES)
    seg = live_ref.shape[1]
    kdims = tuple(d // 2 for d in dims)
    kcount = kdims[0] * kdims[1] * kdims[2]
    my_coarse = cell_id(tuple(me[i] // 2 for i in range(3)), kdims)
    loads = [pltpu.make_async_copy(src, dst, load_sem.at[k]) for k, (src, dst) in enumerate((
        (live_ref, live), (line_ref, blocks.at[0, :, pl.ds(3 * seg, 3 * seg)]),
        (mid_ref, blocks.at[0, :, pl.ds(0, 3 * seg)]),
        (burg_ref, blocks.at[0, :, pl.ds(6 * seg, 3 * seg)]), (pair_ref, pair)))]
    for load in loads:
        load.start()
    barrier = pltpu.get_barrier_semaphore()
    mesh_id = pl.DeviceIdType.MESH

    def at(rep):
        return tuple((me[i] - rep[i] + dims[i]) % dims[i] for i in range(3))

    def peer(step):
        other = (my_coarse + step) % kcount
        coarse = (other // (kdims[1] * kdims[2]), other // kdims[2] % kdims[1], other % kdims[2])
        return tuple(2 * coarse[i] + me[i] % 2 for i in range(3))

    steps = [tuple(r if i == axis else 0 for i in range(3))
             for axis in range(3) for r in reps(dims[axis]) if r != 0]
    parity = tuple(me[i] % 2 for i in range(3))
    my_part = parity[0] * 4 + parity[1] * 2 + parity[2]

    def partner(step):
        bits = (step // 4, step // 2 % 2, step % 2)
        return tuple(me[i] + bits[i] * (1 - 2 * parity[i]) for i in range(3))

    diagonal = (3, 5, 6, 7)
    for rep in steps:
        pl.semaphore_signal(barrier, inc=1, device_id=at(rep), device_id_type=mesh_id)
    for step in diagonal:
        pl.semaphore_signal(barrier, inc=1, device_id=partner(step), device_id_type=mesh_id)

    def greet(step, carry):
        pl.semaphore_signal(barrier, inc=1, device_id=peer(step), device_id_type=mesh_id)
        return carry

    lax.fori_loop(1, kcount, greet, 0)

    held[...] = jnp.zeros_like(held)
    acc[...] = jnp.zeros_like(acc)
    for buf in (basis, weights, feat, tall, high1, low1):
        buf[...] = jnp.zeros_like(buf)
    for load in loads:
        load.wait()

    def row(c):
        return blocks[0, :, c * seg:(c + 1) * seg]

    alive = live[...].astype(F32)
    for c in range(3, 6):
        blocks[0, :, c * seg:(c + 1) * seg] = row(c) * alive
    lane = lax.broadcasted_iota(jnp.int32, (1, 128), 1)
    blocks[0, :, 9 * seg:9 * seg + 128] = jnp.where(lane == 13, jnp.sum(alive, axis=1, keepdims=True), 0.0)
    blocks[0, :, 9 * seg:9 * seg + 13] = pair[...].astype(F32)

    z = [row(c) + ((me[c] % 2) - 1).astype(F32) for c in range(3)]
    terms = [jnp.ones_like(z[0])] + z + [z[a] * z[b] for a in range(3) for b in range(3)]
    for q in range(13):
        basis[q:q + 1] = terms[q]
    for a in range(3):
        for b in range(3):
            weights[3 * a + b:3 * a + b + 1] = row(6 + a) * row(3 + b)
    moments = lax.dot_general(weights[...], basis[...], NT, precision=lax.Precision.HIGHEST,
                              preferred_element_type=F32)
    sub = lax.broadcasted_iota(jnp.int32, moments.shape, 0)
    flat = jnp.where(sub == 0, moments, 0.0)
    for c in range(1, 9):
        flat = flat + pltpu.roll(jnp.where(sub == c, moments, 0.0), 13 * c, 1)
    sums[my_part] = jnp.sum(flat, axis=0, keepdims=True)

    pl.semaphore_wait(barrier, len(steps) + len(diagonal) + kcount - 1)

    def part_copy(step):
        return pltpu.make_async_remote_copy(
            src_ref=sums.at[my_part], dst_ref=sums.at[my_part], send_sem=part_send.at[step],
            recv_sem=part_recv.at[step], device_id=partner(step), device_id_type=mesh_id)

    for step in range(1, 8):
        part_copy(step).start()

    copies = {}

    def send(rep, axis):
        kept = tuple(0 if i == axis else rep[i] for i in range(3))
        moved = tuple(rep[i] if i == axis else 0 for i in range(3))
        slot = slot_index(dims, rep)
        copy = pltpu.make_async_remote_copy(
            src_ref=blocks.at[slot_index(dims, kept)], dst_ref=blocks.at[slot],
            send_sem=send_sem.at[slot], recv_sem=recv_sem.at[slot],
            device_id=at(moved), device_id_type=mesh_id)
        copy.start()
        copies[slot] = copy

    waited = set()

    def arrived(rep):
        if rep not in waited:
            waited.add(rep)
            copies[slot_index(dims, rep)].wait_recv()

    xs, ys, zs = (reps(d)[1:] for d in dims)
    for r in zs:
        send((0, 0, r), 2)
    for r in xs:
        send((r, 0, 0), 0)
    for r in ys:
        send((0, r, 0), 1)

    for r in zs:
        arrived((0, 0, r))
        for a in xs:
            send((a, 0, r), 0)
        for b in ys:
            send((0, b, r), 1)
    for b in ys:
        arrived((0, b, 0))
        for a in xs:
            send((a, b, 0), 0)
    for step in range(1, 8):
        part_copy(step).wait_recv()
    total = sums[0]
    for k in range(1, 8):
        total = total + sums[k]
    table[my_coarse] = total

    def table_copy(step):
        return pltpu.make_async_remote_copy(
            src_ref=table.at[my_coarse], dst_ref=table.at[my_coarse], send_sem=table_send.at[step],
            recv_sem=table_recv.at[step], device_id=peer(step), device_id_type=mesh_id)

    def start_table(step, carry):
        table_copy(step).start()
        return carry

    lax.fori_loop(1, kcount, start_table, 0)

    x = [row(c) - 0.5 for c in range(3)]
    hold_targets(row, x, feat, weights, held)
    rows[...], cols[...] = lay_sources(row, x, feat, weights, tall)
    for r in zs:
        for a in xs:
            arrived((a, 0, r))
            for b in ys:
                send((a, b, r), 1)
    spans = seg // ROWS
    tiles = seg // LANES
    buffers = ((high0, low0), (high1, low1))

    per_turn = 4

    def own_steps(turn, carry):
        for k in range(per_turn):
            step = turn * per_turn + k
            before = jnp.maximum(step - 1, 0)
            strengths(held, rows, step // spans, step % spans, buffers[k % 2])
            gather_force(cols, acc, before // spans, before % spans, buffers[1 - k % 2])
        return carry

    lax.fori_loop(0, tiles * spans // per_turn, own_steps, 0)
    gather_force(cols, acc, tiles - 1, spans - 1, buffers[1])
    def wait_table(step, carry):
        table_copy(step).wait()
        return carry

    lax.fori_loop(1, kcount, wait_table, 0)
    to_scalars = pltpu.make_async_copy(table, table_s, load_sem.at[5])
    to_scalars.start()
    width = seg // 8
    for c in range(9):
        for s in range(8):
            eight[c, s:s + 1] = blocks[0, :, c * seg + s * width:c * seg + (s + 1) * width]
    to_scalars.wait()
    w8 = [eight[6 + a] * eight[3 + b] for a in range(3) for b in range(3)]

    def far_step(k, grads):
        kc = (k // (kdims[1] * kdims[2]), k // kdims[2] % kdims[1], k % kdims[2])
        u = []
        for i in range(3):
            gap = (me[i] - 2 * kc[i] + dims[i] + dims[i] // 2) % dims[i] - dims[i] // 2
            u.append(eight[i] + (gap.astype(F32) - 1.0))
        q = []
        for m in range(13):
            value = table_s[k, 0, m] * w8[0]
            for c in range(1, 9):
                value = value + table_s[k, 0, 13 * c + m] * w8[c]
            q.append(value)
        inv = lax.rsqrt(u[0] * u[0] + u[1] * u[1] + u[2] * u[2] + SPLIT_SQ)
        inv2 = inv * inv
        inv3 = inv2 * inv
        inv5 = inv3 * inv2
        inv7 = inv5 * inv2
        dip = q[1] * u[0] + q[2] * u[1] + q[3] * u[2]
        quad = [q[4 + 3 * a] * u[0] + q[5 + 3 * a] * u[1] + q[6 + 3 * a] * u[2] for a in range(3)]
        form = quad[0] * u[0] + quad[1] * u[1] + quad[2] * u[2]
        trace = q[4] + q[8] + q[12]
        radial = (1.5 * trace - 3.0 * dip) * inv5 - q[0] * inv3 - 7.5 * form * inv7
        return tuple(grads[c] + u[c] * radial + q[1 + c] * inv3 + 3.0 * quad[c] * inv5
                     for c in range(3))

    zero = jnp.zeros((8, width), F32)
    grads = lax.fori_loop(0, kcount, far_step, (zero, zero, zero))
    for c in range(3):
        far[c] = grads[c]
    for rep in [(a, b, r) for r in [0] + zs for a in [0] + xs for b in [0] + ys]:
        if rep != (0, 0, 0):
            arrived(rep)

    for step in range(1, 8):
        part_copy(step).wait_send()
    for copy in copies.values():
        copy.wait_send()
    for slot in range(blocks.shape[0]):
        ctrl[slot] = blocks[slot, :, 9 * seg:9 * seg + 128]


def force_kernel(dims, scalars, blocks, held, own, far, out,
                 feat, wide, tall, rows, cols, high0, low0, high1, low1, acc, todo):
    me = tuple(lax.axis_index(a) for a in AXES)
    tiles = held.shape[0] - 1
    seg = tiles * LANES
    width = seg // 8
    for buf in (feat, wide, tall, high1, low1):
        buf[...] = jnp.zeros_like(buf)
    acc[...] = own[...]
    def list_source(t, carry):
        at, found = carry
        slot = slot_index(dims, (t // 9 - 1, t // 3 % 3 - 1, t % 3 - 1))
        ahead = t > 13
        flag = scalars[jnp.where(ahead, 0, slot), 0,
                       jnp.where(ahead, t - 14, jnp.maximum(12 - t, 0))]
        listed = jnp.logical_and(t != 13, flag > 0.0)
        todo[0, found] = t
        todo[1, found] = at
        size = (scalars[slot, 0, 13].astype(jnp.int32) + (GRAIN - 1)) // GRAIN * GRAIN
        return at + jnp.where(listed, size, 0), found + listed.astype(jnp.int32)

    total, found = lax.fori_loop(0, 27, list_source, (0, 0))
    todo[0, found] = 13
    todo[1, found] = total

    def two_sources(i, carry):
        laid = []
        for k in range(2):
            t, at = todo[0, 2 * i + k], todo[1, 2 * i + k]
            offset = (t // 9 - 1, t // 3 % 3 - 1, t % 3 - 1)
            slot = slot_index(dims, offset)

            def row(c, slot=slot):
                return blocks[slot, :, c * seg:(c + 1) * seg]

            y = [row(c) + (offset[c].astype(F32) - 0.5) for c in range(3)]
            laid.append((at, lay_sources(row, y, feat.at[k], wide.at[k], tall.at[k])))
        for at, (row_part, col_part) in laid:
            here = pl.ds(pl.multiple_of(at, GRAIN), seg)
            rows[here, :] = row_part
            cols[:, here] = col_part
        return carry

    lax.fori_loop(0, (found + 1) // 2, two_sources, 0)
    lane = lax.broadcasted_iota(jnp.int32, (ROWS, 128), 1)
    rows[pl.ds(pl.multiple_of(total, GRAIN), ROWS), :] = (lane == 3).astype(F32).astype(BF16)
    cols[:, pl.ds(pl.multiple_of(total, GRAIN), ROWS)] = jnp.zeros((16, ROWS), BF16)

    my_tiles = (scalars[0, 0, 13].astype(jnp.int32) + (LANES - 1)) // LANES
    spans = (total + (ROWS - 1)) // ROWS
    steps = my_tiles * spans
    buffers = ((high0, low0), (high1, low1))

    def place(step):
        done = step >= steps
        tile = jnp.where(done, tiles, step // spans)
        return tile, jnp.where(done, 0, step % spans)

    def some_steps(first, many):
        for k in range(many):
            strengths(held, rows, *place(first + k), buffers[k % 2])
            gather_force(cols, acc, *place(jnp.maximum(first + k - 1, 0)), buffers[1 - k % 2])

    def many_steps(i, carry):
        some_steps(i * UNROLL, UNROLL)
        return carry

    def two_steps(i, carry):
        some_steps(i * 2, 2)
        return carry

    groups = steps // UNROLL
    pairs = (steps + 1) // 2
    lax.fori_loop(0, groups, many_steps, 0)
    lax.fori_loop(groups * (UNROLL // 2), pairs, two_steps, 0)

    @pl.when(pairs > 0)
    def _():
        gather_force(cols, acc, *place(pairs * 2 - 1), buffers[1])


    slot_id = lax.broadcasted_iota(jnp.int32, (8, width), 0) * width + lax.broadcasted_iota(
        jnp.int32, (8, width), 1)
    alive = (slot_id.astype(F32) < scalars[0, 0, 13]).astype(F32)
    for c in range(3):
        for t in range(tiles):
            turned = acc[t]
            near = (blocks[0, :, c * seg + t * LANES:c * seg + (t + 1) * LANES] - 0.5) * turned[4:5] - (turned[c:c + 1] + turned[8 + c:9 + c] + turned[12 + c:13 + c])
            for s in range(t * LANES // width, (t + 1) * LANES // width):
                inside = slice(s * width - t * LANES, (s + 1) * width - t * LANES)
                out[c, :, s * width:(s + 1) * width] = (near[:, inside] - far[c, s:s + 1]) * alive[s:s + 1]


def on_device(dims, midpoints, line_vectors, burgers, live_mask, pair_list):
    seg = midpoints.shape[4]
    count = dims[0] * dims[1] * dims[2]
    kcount = count // 8
    slots = len(reps(dims[0])) * len(reps(dims[1])) * len(reps(dims[2]))
    vmem = pl.BlockSpec(memory_space=pltpu.VMEM)
    smem = pl.BlockSpec(memory_space=pltpu.SMEM)
    hbm = pl.BlockSpec(memory_space=pltpu.HBM)
    strength_buffer = pltpu.VMEM((PARTS, ROWS, 128), BF16)
    targets = (seg // LANES + 1, 2 * PARTS, 128, 128)
    sums = (seg // LANES + 1, 16, LANES)
    blocks, ctrl, held, own, far = pl.pallas_call(
        functools.partial(gather_kernel, dims),
        out_shape=(jax.ShapeDtypeStruct((slots, 1, 9 * seg + 128), F32),
                   jax.ShapeDtypeStruct((slots, 1, 128), F32),
                   jax.ShapeDtypeStruct(targets, BF16),
                   jax.ShapeDtypeStruct(sums, F32),
                   jax.ShapeDtypeStruct((3, 8, seg // 8), F32)),
        in_specs=[hbm] * 5,
        out_specs=(vmem,) * 5,
        scratch_shapes=[
            pltpu.VMEM((16, seg), F32),
            pltpu.VMEM((128, seg), F32),
            pltpu.VMEM((8, 1, 128), F32),
            pltpu.VMEM((kcount, 1, 128), F32),
            pltpu.SMEM((kcount, 1, 128), F32),
            pltpu.VMEM((9, 8, seg // 8), F32),
            pltpu.VMEM((1, seg), jnp.int32),
            pltpu.VMEM((1, 13), jnp.int32),
            pltpu.VMEM((8, seg), F32),
            pltpu.VMEM((128, seg), F32),
            pltpu.VMEM((seg, 128), BF16),
            pltpu.VMEM((16, seg), BF16),
            *[strength_buffer] * 4,
            pltpu.SemaphoreType.DMA((6,)),
            pltpu.SemaphoreType.DMA((slots,)),
            pltpu.SemaphoreType.DMA((slots,)),
            pltpu.SemaphoreType.DMA((8,)),
            pltpu.SemaphoreType.DMA((8,)),
            pltpu.SemaphoreType.DMA((kcount,)),
            pltpu.SemaphoreType.DMA((kcount,)),
        ],
        compiler_params=pltpu.CompilerParams(collective_id=0, has_side_effects=True),
        name="gather",
    )(*(a.reshape(1, 3 * seg) for a in (midpoints, line_vectors, burgers)),
      live_mask.reshape(1, seg), pair_list.reshape(1, 13))
    out = pl.pallas_call(
        functools.partial(force_kernel, dims),
        out_shape=jax.ShapeDtypeStruct((3, 1, seg), F32),
        in_specs=[smem] + [vmem] * 4,
        out_specs=vmem,
        scratch_shapes=[
            pltpu.VMEM((2, 8, seg), F32),
            pltpu.VMEM((2, 16, seg), F32),
            pltpu.VMEM((2, 128, seg), F32),
            pltpu.VMEM((27 * seg + ROWS, 128), BF16),
            pltpu.VMEM((16, 27 * seg + ROWS), BF16),
            *[strength_buffer] * 4,
            pltpu.VMEM(sums, F32),
            pltpu.SMEM((2, 32), jnp.int32),
        ],
        compiler_params=pltpu.CompilerParams(vmem_limit_bytes=60 * 2**20),
        name="forces",
    )(ctrl, blocks, held, own, far)
    return out.reshape(3, 1, 1, 1, seg)


def solution(mesh):
    dims = tuple(mesh.shape[a] for a in AXES)
    placed = (
        P(None, "gx", "gy", "gz", None),
        P(None, "gx", "gy", "gz", None),
        P(None, "gx", "gy", "gz", None),
        P("gx", "gy", "gz", None),
        P(None, "gx", "gy", "gz"),
    )
    return jax.shard_map(
        functools.partial(on_device, dims),
        mesh=mesh,
        in_specs=placed,
        out_specs=P(None, "gx", "gy", "gz", None),
        check_vma=False,
    )
```

```python
import functools

import jax
import jax.numpy as jnp
from jax import lax
from jax.experimental import pallas as pl
from jax.experimental.pallas import tpu as pltpu
from jax.sharding import PartitionSpec as P

AXES = ("gx", "gy", "gz")
CORE_SQ = 0.1 * 0.1
SPLIT_SQ = 2.0 * 2.0
LANES = 256
ROWS = 512
CHUNK = 256
UNROLL = 12
PARTS = LANES // 128
GRAIN = 128
F32 = jnp.float32
BF16 = jnp.bfloat16
NT = (((1,), (1,)), ((), ()))


def reps(size):
    return [0] if size == 1 else [0, 1] if size == 2 else [0, 1, -1]


def cell_id(cell, dims):
    return (cell[0] * dims[1] + cell[1]) * dims[2] + cell[2]


def split3(value):
    high = value.astype(BF16).astype(F32)
    rest = value - high
    middle = rest.astype(BF16).astype(F32)
    return high, middle, rest - middle


def split_coupling(row, wide):
    for a in range(3):
        for b in range(3):
            wide[3 * a + b:3 * a + b + 1] = row(6 + a) * row(3 + b)
    whole = wide[...]
    high = whole.astype(BF16).astype(F32)
    return high, whole - high


def hold_targets(row, x, feat, wide, held):
    for c in range(3):
        feat[c:c + 1] = -2.0 * x[c]
    feat[3:4] = jnp.ones_like(x[0])
    feat[4:5] = x[0] * x[0] + x[1] * x[1] + x[2] * x[2] + CORE_SQ
    high, middle, low = split3(feat[...])
    whigh, wlow = split_coupling(row, wide)
    distance = jnp.concatenate([high, high, high, middle, middle, low], axis=0).astype(BF16)
    coupling = jnp.concatenate([whigh, whigh, wlow], axis=0).astype(BF16)
    for t in range(held.shape[0] - 1):
        for i in range(PARTS):
            cut = slice(t * LANES + i * 128, t * LANES + (i + 1) * 128)
            held[t, i, 0:48] = distance[:, cut]
            held[t, PARTS + i, 48:96] = coupling[:, cut]


def lay_sources(row, y, feat, wide, tall):
    for c in range(3):
        feat[c:c + 1] = y[c]
    feat[3:4] = y[0] * y[0] + y[1] * y[1] + y[2] * y[2]
    feat[4:5] = jnp.ones_like(y[0])
    high, middle, low = split3(feat[...])
    for k, part in enumerate((high, middle, low, high, middle, high)):
        tall[8 * k:8 * k + 8] = part
    whigh, wlow = split_coupling(row, wide)
    tall[48:64] = whigh
    tall[64:80] = wlow
    tall[80:96] = whigh
    return (jnp.transpose(tall[...].astype(BF16)),
            jnp.concatenate([high, middle + pltpu.roll(low, 4, 0)], axis=0).astype(BF16))


def strengths(held, rows, tile, span, to):
    w = jnp.concatenate([held[tile, i] for i in range(2 * PARTS)], axis=1)
    for u in range(0, ROWS, CHUNK):
        lhs = rows[pl.ds(pl.multiple_of(span * ROWS + u, CHUNK), CHUNK), :]
        product = jnp.dot(lhs, w, preferred_element_type=F32)
        for i in range(PARTS):
            near = product[:, i * 128:(i + 1) * 128]
            pull = product[:, LANES + i * 128:LANES + (i + 1) * 128]
            inner = lax.rsqrt(near)
            outer = lax.rsqrt(near + (SPLIT_SQ - CORE_SQ))
            strength = pull * (inner * inner * inner - outer * outer * outer)
            top = strength.astype(BF16)
            to[0][i, u:u + CHUNK] = top
            to[1][i, u:u + CHUNK] = (strength - top.astype(F32)).astype(BF16)


def gather_force(cols, acc, tile, span, of):
    part = cols[:, pl.ds(pl.multiple_of(span * ROWS, ROWS), ROWS)]
    top, rest = (jnp.concatenate([buf[i] for i in range(PARTS)], axis=1) for buf in of)
    acc[tile] += (jnp.dot(part, top, preferred_element_type=F32)
                  + jnp.dot(part, rest, preferred_element_type=F32))


def slot_index(dims, rep):
    slot = 0
    for i in range(3):
        base = min(dims[i], 3)
        slot = slot * base + (rep[i] + base) % base
    return slot


def gather_kernel(dims, mid_ref, line_ref, burg_ref, live_ref, pair_ref, blocks, ctrl, held, acc, far,
                  weights, basis, sums, table, table_s, eight, live, pair, feat, tall, rows, cols, high0, low0, high1, low1,
                  load_sem, send_sem, recv_sem, part_send, part_recv, table_send, table_recv):
    me = tuple(lax.axis_index(a) for a in AXES)
    seg = live_ref.shape[1]
    kdims = tuple(d // 2 for d in dims)
    kcount = kdims[0] * kdims[1] * kdims[2]
    my_coarse = cell_id(tuple(me[i] // 2 for i in range(3)), kdims)
    loads = [pltpu.make_async_copy(src, dst, load_sem.at[k]) for k, (src, dst) in enumerate((
        (live_ref, live), (line_ref, blocks.at[0, :, pl.ds(3 * seg, 3 * seg)]),
        (mid_ref, blocks.at[0, :, pl.ds(0, 3 * seg)]),
        (burg_ref, blocks.at[0, :, pl.ds(6 * seg, 3 * seg)]), (pair_ref, pair)))]
    for load in loads:
        load.start()
    barrier = pltpu.get_barrier_semaphore()
    mesh_id = pl.DeviceIdType.MESH

    def at(rep):
        return tuple((me[i] - rep[i] + dims[i]) % dims[i] for i in range(3))

    def peer(step):
        other = (my_coarse + step) % kcount
        coarse = (other // (kdims[1] * kdims[2]), other // kdims[2] % kdims[1], other % kdims[2])
        return tuple(2 * coarse[i] + me[i] % 2 for i in range(3))

    steps = [tuple(r if i == axis else 0 for i in range(3))
             for axis in range(3) for r in reps(dims[axis]) if r != 0]
    parity = tuple(me[i] % 2 for i in range(3))
    my_part = parity[0] * 4 + parity[1] * 2 + parity[2]

    def partner(step):
        bits = (step // 4, step // 2 % 2, step % 2)
        return tuple(me[i] + bits[i] * (1 - 2 * parity[i]) for i in range(3))

    diagonal = (3, 5, 6, 7)
    for rep in steps:
        pl.semaphore_signal(barrier, inc=1, device_id=at(rep), device_id_type=mesh_id)
    for step in diagonal:
        pl.semaphore_signal(barrier, inc=1, device_id=partner(step), device_id_type=mesh_id)

    def greet(step, carry):
        pl.semaphore_signal(barrier, inc=1, device_id=peer(step), device_id_type=mesh_id)
        return carry

    lax.fori_loop(1, kcount, greet, 0)

    held[...] = jnp.zeros_like(held)
    acc[...] = jnp.zeros_like(acc)
    for buf in (basis, weights, feat, tall, high1, low1):
        buf[...] = jnp.zeros_like(buf)
    for load in loads:
        load.wait()

    def row(c):
        return blocks[0, :, c * seg:(c + 1) * seg]

    alive = live[...].astype(F32)
    for c in range(3, 6):
        blocks[0, :, c * seg:(c + 1) * seg] = row(c) * alive
    lane = lax.broadcasted_iota(jnp.int32, (1, 128), 1)
    blocks[0, :, 9 * seg:9 * seg + 128] = jnp.where(lane == 13, jnp.sum(alive, axis=1, keepdims=True), 0.0)
    blocks[0, :, 9 * seg:9 * seg + 13] = pair[...].astype(F32)

    z = [row(c) + ((me[c] % 2) - 1).astype(F32) for c in range(3)]
    terms = [jnp.ones_like(z[0])] + z + [z[a] * z[b] for a in range(3) for b in range(3)]
    for q in range(13):
        basis[q:q + 1] = terms[q]
    for a in range(3):
        for b in range(3):
            weights[3 * a + b:3 * a + b + 1] = row(6 + a) * row(3 + b)
    moments = lax.dot_general(weights[...], basis[...], NT, precision=lax.Precision.HIGHEST,
                              preferred_element_type=F32)
    sub = lax.broadcasted_iota(jnp.int32, moments.shape, 0)
    flat = jnp.where(sub == 0, moments, 0.0)
    for c in range(1, 9):
        flat = flat + pltpu.roll(jnp.where(sub == c, moments, 0.0), 13 * c, 1)
    sums[my_part] = jnp.sum(flat, axis=0, keepdims=True)

    pl.semaphore_wait(barrier, len(steps) + len(diagonal) + kcount - 1)

    def part_copy(step):
        return pltpu.make_async_remote_copy(
            src_ref=sums.at[my_part], dst_ref=sums.at[my_part], send_sem=part_send.at[step],
            recv_sem=part_recv.at[step], device_id=partner(step), device_id_type=mesh_id)

    for step in range(1, 8):
        part_copy(step).start()

    copies = {}

    def send(rep, axis):
        kept = tuple(0 if i == axis else rep[i] for i in range(3))
        moved = tuple(rep[i] if i == axis else 0 for i in range(3))
        slot = slot_index(dims, rep)
        copy = pltpu.make_async_remote_copy(
            src_ref=blocks.at[slot_index(dims, kept)], dst_ref=blocks.at[slot],
            send_sem=send_sem.at[slot], recv_sem=recv_sem.at[slot],
            device_id=at(moved), device_id_type=mesh_id)
        copy.start()
        copies[slot] = copy

    waited = set()

    def arrived(rep):
        if rep not in waited:
            waited.add(rep)
            copies[slot_index(dims, rep)].wait_recv()

    xs, ys, zs = (reps(d)[1:] for d in dims)
    for r in zs:
        send((0, 0, r), 2)
    for r in xs:
        send((r, 0, 0), 0)
    for r in ys:
        send((0, r, 0), 1)

    x = [row(c) - 0.5 for c in range(3)]
    hold_targets(row, x, feat, weights, held)
    rows[...], cols[...] = lay_sources(row, x, feat, weights, tall)
    spans = seg // ROWS
    tiles = seg // LANES
    buffers = ((high0, low0), (high1, low1))

    per_turn = 4

    def own_steps(turn, carry):
        for k in range(per_turn):
            step = turn * per_turn + k
            before = jnp.maximum(step - 1, 0)
            strengths(held, rows, step // spans, step % spans, buffers[k % 2])
            gather_force(cols, acc, before // spans, before % spans, buffers[1 - k % 2])
        return carry

    lax.fori_loop(0, tiles * spans // per_turn, own_steps, 0)
    for r in zs:
        arrived((0, 0, r))
        for a in xs:
            send((a, 0, r), 0)
        for b in ys:
            send((0, b, r), 1)
    for b in ys:
        arrived((0, b, 0))
        for a in xs:
            send((a, b, 0), 0)
    for step in range(1, 8):
        part_copy(step).wait_recv()
    total = sums[0]
    for k in range(1, 8):
        total = total + sums[k]
    table[my_coarse] = total

    def table_copy(step):
        return pltpu.make_async_remote_copy(
            src_ref=table.at[my_coarse], dst_ref=table.at[my_coarse], send_sem=table_send.at[step],
            recv_sem=table_recv.at[step], device_id=peer(step), device_id_type=mesh_id)

    def start_table(step, carry):
        table_copy(step).start()
        return carry

    lax.fori_loop(1, kcount, start_table, 0)

    for r in zs:
        for a in xs:
            arrived((a, 0, r))
            for b in ys:
                send((a, b, r), 1)
    gather_force(cols, acc, tiles - 1, spans - 1, buffers[1])
    def wait_table(step, carry):
        table_copy(step).wait()
        return carry

    lax.fori_loop(1, kcount, wait_table, 0)
    to_scalars = pltpu.make_async_copy(table, table_s, load_sem.at[5])
    to_scalars.start()
    width = seg // 8
    for c in range(9):
        for s in range(8):
            eight[c, s:s + 1] = blocks[0, :, c * seg + s * width:c * seg + (s + 1) * width]
    to_scalars.wait()
    w8 = [eight[6 + a] * eight[3 + b] for a in range(3) for b in range(3)]

    def far_step(k, grads):
        kc = (k // (kdims[1] * kdims[2]), k // kdims[2] % kdims[1], k % kdims[2])
        u = []
        for i in range(3):
            gap = (me[i] - 2 * kc[i] + dims[i] + dims[i] // 2) % dims[i] - dims[i] // 2
            u.append(eight[i] + (gap.astype(F32) - 1.0))
        q = []
        for m in range(13):
            value = table_s[k, 0, m] * w8[0]
            for c in range(1, 9):
                value = value + table_s[k, 0, 13 * c + m] * w8[c]
            q.append(value)
        inv = lax.rsqrt(u[0] * u[0] + u[1] * u[1] + u[2] * u[2] + SPLIT_SQ)
        inv2 = inv * inv
        inv3 = inv2 * inv
        inv5 = inv3 * inv2
        inv7 = inv5 * inv2
        dip = q[1] * u[0] + q[2] * u[1] + q[3] * u[2]
        quad = [q[4 + 3 * a] * u[0] + q[5 + 3 * a] * u[1] + q[6 + 3 * a] * u[2] for a in range(3)]
        form = quad[0] * u[0] + quad[1] * u[1] + quad[2] * u[2]
        trace = q[4] + q[8] + q[12]
        radial = (1.5 * trace - 3.0 * dip) * inv5 - q[0] * inv3 - 7.5 * form * inv7
        return tuple(grads[c] + u[c] * radial + q[1 + c] * inv3 + 3.0 * quad[c] * inv5
                     for c in range(3))

    zero = jnp.zeros((8, width), F32)
    grads = lax.fori_loop(0, kcount, far_step, (zero, zero, zero))
    for c in range(3):
        far[c] = grads[c]
    for rep in [(a, b, r) for r in [0] + zs for a in [0] + xs for b in [0] + ys]:
        if rep != (0, 0, 0):
            arrived(rep)

    for step in range(1, 8):
        part_copy(step).wait_send()
    for copy in copies.values():
        copy.wait_send()
    for slot in range(blocks.shape[0]):
        ctrl[slot] = blocks[slot, :, 9 * seg:9 * seg + 128]


def force_kernel(dims, scalars, blocks, held, own, far, out,
                 feat, wide, tall, rows, cols, high0, low0, high1, low1, acc, todo):
    me = tuple(lax.axis_index(a) for a in AXES)
    tiles = held.shape[0] - 1
    seg = tiles * LANES
    width = seg // 8
    for buf in (feat, wide, tall, high1, low1):
        buf[...] = jnp.zeros_like(buf)
    acc[...] = own[...]
    def list_source(t, carry):
        at, found = carry
        slot = slot_index(dims, (t // 9 - 1, t // 3 % 3 - 1, t % 3 - 1))
        ahead = t > 13
        flag = scalars[jnp.where(ahead, 0, slot), 0,
                       jnp.where(ahead, t - 14, jnp.maximum(12 - t, 0))]
        listed = jnp.logical_and(t != 13, flag > 0.0)
        todo[0, found] = t
        todo[1, found] = at
        size = (scalars[slot, 0, 13].astype(jnp.int32) + (GRAIN - 1)) // GRAIN * GRAIN
        return at + jnp.where(listed, size, 0), found + listed.astype(jnp.int32)

    total, found = lax.fori_loop(0, 27, list_source, (0, 0))
    todo[0, found] = 13
    todo[1, found] = total

    def two_sources(i, carry):
        laid = []
        for k in range(2):
            t, at = todo[0, 2 * i + k], todo[1, 2 * i + k]
            offset = (t // 9 - 1, t // 3 % 3 - 1, t % 3 - 1)
            slot = slot_index(dims, offset)

            def row(c, slot=slot):
                return blocks[slot, :, c * seg:(c + 1) * seg]

            y = [row(c) + (offset[c].astype(F32) - 0.5) for c in range(3)]
            laid.append((at, lay_sources(row, y, feat.at[k], wide.at[k], tall.at[k])))
        for at, (row_part, col_part) in laid:
            here = pl.ds(pl.multiple_of(at, GRAIN), seg)
            rows[here, :] = row_part
            cols[:, here] = col_part
        return carry

    lax.fori_loop(0, (found + 1) // 2, two_sources, 0)
    lane = lax.broadcasted_iota(jnp.int32, (ROWS, 128), 1)
    rows[pl.ds(pl.multiple_of(total, GRAIN), ROWS), :] = (lane == 3).astype(F32).astype(BF16)
    cols[:, pl.ds(pl.multiple_of(total, GRAIN), ROWS)] = jnp.zeros((16, ROWS), BF16)

    my_tiles = (scalars[0, 0, 13].astype(jnp.int32) + (LANES - 1)) // LANES
    spans = (total + (ROWS - 1)) // ROWS
    steps = my_tiles * spans
    buffers = ((high0, low0), (high1, low1))

    def place(step):
        done = step >= steps
        tile = jnp.where(done, tiles, step // spans)
        return tile, jnp.where(done, 0, step % spans)

    def some_steps(first, many):
        for k in range(many):
            strengths(held, rows, *place(first + k), buffers[k % 2])
            gather_force(cols, acc, *place(jnp.maximum(first + k - 1, 0)), buffers[1 - k % 2])

    def many_steps(i, carry):
        some_steps(i * UNROLL, UNROLL)
        return carry

    def two_steps(i, carry):
        some_steps(i * 2, 2)
        return carry

    def four_steps(i, carry):
        some_steps(i * 4, 4)
        return carry

    groups = steps // UNROLL
    fours = steps // 4
    pairs = (steps + 1) // 2
    lax.fori_loop(0, groups, many_steps, 0)
    lax.fori_loop(groups * (UNROLL // 4), fours, four_steps, 0)
    lax.fori_loop(fours * 2, pairs, two_steps, 0)

    @pl.when(pairs > 0)
    def _():
        gather_force(cols, acc, *place(pairs * 2 - 1), buffers[1])


    slot_id = lax.broadcasted_iota(jnp.int32, (8, width), 0) * width + lax.broadcasted_iota(
        jnp.int32, (8, width), 1)
    alive = (slot_id.astype(F32) < scalars[0, 0, 13]).astype(F32)
    for c in range(3):
        for t in range(tiles):
            turned = acc[t]
            near = (blocks[0, :, c * seg + t * LANES:c * seg + (t + 1) * LANES] - 0.5) * turned[4:5] - (turned[c:c + 1] + turned[8 + c:9 + c] + turned[12 + c:13 + c])
            for s in range(t * LANES // width, (t + 1) * LANES // width):
                inside = slice(s * width - t * LANES, (s + 1) * width - t * LANES)
                out[c, :, s * width:(s + 1) * width] = (near[:, inside] - far[c, s:s + 1]) * alive[s:s + 1]


def on_device(dims, midpoints, line_vectors, burgers, live_mask, pair_list):
    seg = midpoints.shape[4]
    count = dims[0] * dims[1] * dims[2]
    kcount = count // 8
    slots = len(reps(dims[0])) * len(reps(dims[1])) * len(reps(dims[2]))
    vmem = pl.BlockSpec(memory_space=pltpu.VMEM)
    smem = pl.BlockSpec(memory_space=pltpu.SMEM)
    hbm = pl.BlockSpec(memory_space=pltpu.HBM)
    strength_buffer = pltpu.VMEM((PARTS, ROWS, 128), BF16)
    targets = (seg // LANES + 1, 2 * PARTS, 128, 128)
    sums = (seg // LANES + 1, 16, LANES)
    blocks, ctrl, held, own, far = pl.pallas_call(
        functools.partial(gather_kernel, dims),
        out_shape=(jax.ShapeDtypeStruct((slots, 1, 9 * seg + 128), F32),
                   jax.ShapeDtypeStruct((slots, 1, 128), F32),
                   jax.ShapeDtypeStruct(targets, BF16),
                   jax.ShapeDtypeStruct(sums, F32),
                   jax.ShapeDtypeStruct((3, 8, seg // 8), F32)),
        in_specs=[hbm] * 5,
        out_specs=(vmem,) * 5,
        scratch_shapes=[
            pltpu.VMEM((16, seg), F32),
            pltpu.VMEM((128, seg), F32),
            pltpu.VMEM((8, 1, 128), F32),
            pltpu.VMEM((kcount, 1, 128), F32),
            pltpu.SMEM((kcount, 1, 128), F32),
            pltpu.VMEM((9, 8, seg // 8), F32),
            pltpu.VMEM((1, seg), jnp.int32),
            pltpu.VMEM((1, 13), jnp.int32),
            pltpu.VMEM((8, seg), F32),
            pltpu.VMEM((128, seg), F32),
            pltpu.VMEM((seg, 128), BF16),
            pltpu.VMEM((16, seg), BF16),
            *[strength_buffer] * 4,
            pltpu.SemaphoreType.DMA((6,)),
            pltpu.SemaphoreType.DMA((slots,)),
            pltpu.SemaphoreType.DMA((slots,)),
            pltpu.SemaphoreType.DMA((8,)),
            pltpu.SemaphoreType.DMA((8,)),
            pltpu.SemaphoreType.DMA((kcount,)),
            pltpu.SemaphoreType.DMA((kcount,)),
        ],
        compiler_params=pltpu.CompilerParams(collective_id=0, has_side_effects=True),
        name="gather",
    )(*(a.reshape(1, 3 * seg) for a in (midpoints, line_vectors, burgers)),
      live_mask.reshape(1, seg), pair_list.reshape(1, 13))
    out = pl.pallas_call(
        functools.partial(force_kernel, dims),
        out_shape=jax.ShapeDtypeStruct((3, 1, seg), F32),
        in_specs=[smem] + [vmem] * 4,
        out_specs=vmem,
        scratch_shapes=[
            pltpu.VMEM((2, 8, seg), F32),
            pltpu.VMEM((2, 16, seg), F32),
            pltpu.VMEM((2, 128, seg), F32),
            pltpu.VMEM((27 * seg + ROWS, 128), BF16),
            pltpu.VMEM((16, 27 * seg + ROWS), BF16),
            *[strength_buffer] * 4,
            pltpu.VMEM(sums, F32),
            pltpu.SMEM((2, 32), jnp.int32),
        ],
        compiler_params=pltpu.CompilerParams(vmem_limit_bytes=60 * 2**20),
        name="forces",
    )(ctrl, blocks, held, own, far)
    return out.reshape(3, 1, 1, 1, seg)


def solution(mesh):
    dims = tuple(mesh.shape[a] for a in AXES)
    placed = (
        P(None, "gx", "gy", "gz", None),
        P(None, "gx", "gy", "gz", None),
        P(None, "gx", "gy", "gz", None),
        P("gx", "gy", "gz", None),
        P(None, "gx", "gy", "gz"),
    )
    return jax.shard_map(
        functools.partial(on_device, dims),
        mesh=mesh,
        in_specs=placed,
        out_specs=P(None, "gx", "gy", "gz", None),
        check_vma=False,
    )
```

```python
import functools

import jax
import jax.numpy as jnp
from jax import lax
from jax.experimental import pallas as pl
from jax.experimental.pallas import tpu as pltpu
from jax.sharding import PartitionSpec as P

AXES = ("gx", "gy", "gz")
CORE_SQ = 0.1 * 0.1
SPLIT_SQ = 2.0 * 2.0
LANES = 256
ROWS = 512
CHUNK = 256
UNROLL = 16
PARTS = LANES // 128
GRAIN = 128
F32 = jnp.float32
BF16 = jnp.bfloat16
NT = (((1,), (1,)), ((), ()))


def reps(size):
    return [0] if size == 1 else [0, 1] if size == 2 else [0, 1, -1]


def cell_id(cell, dims):
    return (cell[0] * dims[1] + cell[1]) * dims[2] + cell[2]


def split3(value):
    high = value.astype(BF16).astype(F32)
    rest = value - high
    middle = rest.astype(BF16).astype(F32)
    return high, middle, rest - middle


def split_coupling(row, wide):
    for a in range(3):
        for b in range(3):
            wide[3 * a + b:3 * a + b + 1] = row(6 + a) * row(3 + b)
    whole = wide[...]
    high = whole.astype(BF16).astype(F32)
    return high, whole - high


def hold_targets(row, x, feat, wide, held):
    for c in range(3):
        feat[c:c + 1] = -2.0 * x[c]
    feat[3:4] = jnp.ones_like(x[0])
    feat[4:5] = x[0] * x[0] + x[1] * x[1] + x[2] * x[2] + CORE_SQ
    high, middle, low = split3(feat[...])
    whigh, wlow = split_coupling(row, wide)
    distance = jnp.concatenate([high, high, high, middle, middle, low], axis=0).astype(BF16)
    coupling = jnp.concatenate([whigh, whigh, wlow], axis=0).astype(BF16)
    for t in range(held.shape[0] - 1):
        for i in range(PARTS):
            cut = slice(t * LANES + i * 128, t * LANES + (i + 1) * 128)
            held[t, i, 0:48] = distance[:, cut]
            held[t, PARTS + i, 48:96] = coupling[:, cut]


def lay_sources(row, y, feat, wide, tall):
    for c in range(3):
        feat[c:c + 1] = y[c]
    feat[3:4] = y[0] * y[0] + y[1] * y[1] + y[2] * y[2]
    feat[4:5] = jnp.ones_like(y[0])
    high, middle, low = split3(feat[...])
    for k, part in enumerate((high, middle, low, high, middle, high)):
        tall[8 * k:8 * k + 8] = part
    whigh, wlow = split_coupling(row, wide)
    tall[48:64] = whigh
    tall[64:80] = wlow
    tall[80:96] = whigh
    return (jnp.transpose(tall[...].astype(BF16)),
            jnp.concatenate([high, middle + pltpu.roll(low, 4, 0)], axis=0).astype(BF16))


def strengths(held, rows, tile, span, to):
    w = jnp.concatenate([held[tile, i] for i in range(2 * PARTS)], axis=1)
    for u in range(0, ROWS, CHUNK):
        lhs = rows[pl.ds(pl.multiple_of(span * ROWS + u, CHUNK), CHUNK), :]
        product = jnp.dot(lhs, w, preferred_element_type=F32)
        for i in range(PARTS):
            near = product[:, i * 128:(i + 1) * 128]
            pull = product[:, LANES + i * 128:LANES + (i + 1) * 128]
            inner = lax.rsqrt(near)
            outer = lax.rsqrt(near + (SPLIT_SQ - CORE_SQ))
            strength = pull * (inner * inner * inner - outer * outer * outer)
            top = strength.astype(BF16)
            to[0][i, u:u + CHUNK] = top
            to[1][i, u:u + CHUNK] = (strength - top.astype(F32)).astype(BF16)


def gather_force(cols, acc, tile, span, of):
    part = cols[:, pl.ds(pl.multiple_of(span * ROWS, ROWS), ROWS)]
    top, rest = (jnp.concatenate([buf[i] for i in range(PARTS)], axis=1) for buf in of)
    acc[tile] += (jnp.dot(part, top, preferred_element_type=F32)
                  + jnp.dot(part, rest, preferred_element_type=F32))


def slot_index(dims, rep):
    slot = 0
    for i in range(3):
        base = min(dims[i], 3)
        slot = slot * base + (rep[i] + base) % base
    return slot


def gather_kernel(dims, mid_ref, line_ref, burg_ref, live_ref, pair_ref, blocks, ctrl, held, acc, far,
                  weights, basis, sums, table, table_s, eight, live, pair, feat, tall, rows, cols, high0, low0, high1, low1,
                  load_sem, send_sem, recv_sem, part_send, part_recv, table_send, table_recv):
    me = tuple(lax.axis_index(a) for a in AXES)
    seg = live_ref.shape[1]
    kdims = tuple(d // 2 for d in dims)
    kcount = kdims[0] * kdims[1] * kdims[2]
    my_coarse = cell_id(tuple(me[i] // 2 for i in range(3)), kdims)
    loads = [pltpu.make_async_copy(src, dst, load_sem.at[k]) for k, (src, dst) in enumerate((
        (live_ref, live), (line_ref, blocks.at[0, :, pl.ds(3 * seg, 3 * seg)]),
        (mid_ref, blocks.at[0, :, pl.ds(0, 3 * seg)]),
        (burg_ref, blocks.at[0, :, pl.ds(6 * seg, 3 * seg)]), (pair_ref, pair)))]
    for load in loads:
        load.start()
    barrier = pltpu.get_barrier_semaphore()
    mesh_id = pl.DeviceIdType.MESH

    def at(rep):
        return tuple((me[i] - rep[i] + dims[i]) % dims[i] for i in range(3))

    def peer(step):
        other = (my_coarse + step) % kcount
        coarse = (other // (kdims[1] * kdims[2]), other // kdims[2] % kdims[1], other % kdims[2])
        return tuple(2 * coarse[i] + me[i] % 2 for i in range(3))

    steps = [tuple(r if i == axis else 0 for i in range(3))
             for axis in range(3) for r in reps(dims[axis]) if r != 0]
    parity = tuple(me[i] % 2 for i in range(3))
    my_part = parity[0] * 4 + parity[1] * 2 + parity[2]

    def partner(step):
        bits = (step // 4, step // 2 % 2, step % 2)
        return tuple(me[i] + bits[i] * (1 - 2 * parity[i]) for i in range(3))

    diagonal = (3, 5, 6, 7)
    for rep in steps:
        pl.semaphore_signal(barrier, inc=1, device_id=at(rep), device_id_type=mesh_id)
    for step in diagonal:
        pl.semaphore_signal(barrier, inc=1, device_id=partner(step), device_id_type=mesh_id)

    def greet(step, carry):
        pl.semaphore_signal(barrier, inc=1, device_id=peer(step), device_id_type=mesh_id)
        return carry

    lax.fori_loop(1, kcount, greet, 0)

    held[...] = jnp.zeros_like(held)
    acc[...] = jnp.zeros_like(acc)
    for buf in (basis, weights, feat, tall, high1, low1):
        buf[...] = jnp.zeros_like(buf)
    for load in loads:
        load.wait()

    def row(c):
        return blocks[0, :, c * seg:(c + 1) * seg]

    alive = live[...].astype(F32)
    for c in range(3, 6):
        blocks[0, :, c * seg:(c + 1) * seg] = row(c) * alive
    lane = lax.broadcasted_iota(jnp.int32, (1, 128), 1)
    blocks[0, :, 9 * seg:9 * seg + 128] = jnp.where(lane == 13, jnp.sum(alive, axis=1, keepdims=True), 0.0)
    blocks[0, :, 9 * seg:9 * seg + 13] = pair[...].astype(F32)

    z = [row(c) + ((me[c] % 2) - 1).astype(F32) for c in range(3)]
    terms = [jnp.ones_like(z[0])] + z + [z[a] * z[b] for a in range(3) for b in range(3)]
    for q in range(13):
        basis[q:q + 1] = terms[q]
    for a in range(3):
        for b in range(3):
            weights[3 * a + b:3 * a + b + 1] = row(6 + a) * row(3 + b)
    moments = lax.dot_general(weights[...], basis[...], NT, precision=lax.Precision.HIGHEST,
                              preferred_element_type=F32)
    sub = lax.broadcasted_iota(jnp.int32, moments.shape, 0)
    flat = jnp.where(sub == 0, moments, 0.0)
    for c in range(1, 9):
        flat = flat + pltpu.roll(jnp.where(sub == c, moments, 0.0), 13 * c, 1)
    sums[my_part] = jnp.sum(flat, axis=0, keepdims=True)

    pl.semaphore_wait(barrier, len(steps) + len(diagonal) + kcount - 1)

    def part_copy(step):
        return pltpu.make_async_remote_copy(
            src_ref=sums.at[my_part], dst_ref=sums.at[my_part], send_sem=part_send.at[step],
            recv_sem=part_recv.at[step], device_id=partner(step), device_id_type=mesh_id)

    for step in range(1, 8):
        part_copy(step).start()

    copies = {}

    def send(rep, axis):
        kept = tuple(0 if i == axis else rep[i] for i in range(3))
        moved = tuple(rep[i] if i == axis else 0 for i in range(3))
        slot = slot_index(dims, rep)
        copy = pltpu.make_async_remote_copy(
            src_ref=blocks.at[slot_index(dims, kept)], dst_ref=blocks.at[slot],
            send_sem=send_sem.at[slot], recv_sem=recv_sem.at[slot],
            device_id=at(moved), device_id_type=mesh_id)
        copy.start()
        copies[slot] = copy

    waited = set()

    def arrived(rep):
        if rep not in waited:
            waited.add(rep)
            copies[slot_index(dims, rep)].wait_recv()

    xs, ys, zs = (reps(d)[1:] for d in dims)
    for r in zs:
        send((0, 0, r), 2)
    for r in xs:
        send((r, 0, 0), 0)
    for r in ys:
        send((0, r, 0), 1)

    x = [row(c) - 0.5 for c in range(3)]
    hold_targets(row, x, feat, weights, held)
    rows[...], cols[...] = lay_sources(row, x, feat, weights, tall)
    spans = seg // ROWS
    tiles = seg // LANES
    buffers = ((high0, low0), (high1, low1))

    per_turn = 4

    def own_steps(turn, carry):
        for k in range(per_turn):
            step = turn * per_turn + k
            before = jnp.maximum(step - 1, 0)
            strengths(held, rows, step // spans, step % spans, buffers[k % 2])
            gather_force(cols, acc, before // spans, before % spans, buffers[1 - k % 2])
        return carry

    lax.fori_loop(0, tiles * spans // per_turn, own_steps, 0)
    for r in zs:
        arrived((0, 0, r))
        for a in xs:
            send((a, 0, r), 0)
        for b in ys:
            send((0, b, r), 1)
    for b in ys:
        arrived((0, b, 0))
        for a in xs:
            send((a, b, 0), 0)
    for step in range(1, 8):
        part_copy(step).wait_recv()
    total = sums[0]
    for k in range(1, 8):
        total = total + sums[k]
    table[my_coarse] = total

    def table_copy(step):
        return pltpu.make_async_remote_copy(
            src_ref=table.at[my_coarse], dst_ref=table.at[my_coarse], send_sem=table_send.at[step],
            recv_sem=table_recv.at[step], device_id=peer(step), device_id_type=mesh_id)

    def start_table(step, carry):
        table_copy(step).start()
        return carry

    lax.fori_loop(1, kcount, start_table, 0)

    for r in zs:
        for a in xs:
            arrived((a, 0, r))
            for b in ys:
                send((a, b, r), 1)
    gather_force(cols, acc, tiles - 1, spans - 1, buffers[1])
    def wait_table(step, carry):
        table_copy(step).wait()
        return carry

    lax.fori_loop(1, kcount, wait_table, 0)
    to_scalars = pltpu.make_async_copy(table, table_s, load_sem.at[5])
    to_scalars.start()
    width = seg // 8
    for c in range(9):
        for s in range(8):
            eight[c, s:s + 1] = blocks[0, :, c * seg + s * width:c * seg + (s + 1) * width]
    to_scalars.wait()
    w8 = [eight[6 + a] * eight[3 + b] for a in range(3) for b in range(3)]

    def far_step(k, grads):
        kc = (k // (kdims[1] * kdims[2]), k // kdims[2] % kdims[1], k % kdims[2])
        u = []
        for i in range(3):
            gap = (me[i] - 2 * kc[i] + dims[i] + dims[i] // 2) % dims[i] - dims[i] // 2
            u.append(eight[i] + (gap.astype(F32) - 1.0))
        q = []
        for m in range(13):
            value = table_s[k, 0, m] * w8[0]
            for c in range(1, 9):
                value = value + table_s[k, 0, 13 * c + m] * w8[c]
            q.append(value)
        inv = lax.rsqrt(u[0] * u[0] + u[1] * u[1] + u[2] * u[2] + SPLIT_SQ)
        inv2 = inv * inv
        inv3 = inv2 * inv
        inv5 = inv3 * inv2
        inv7 = inv5 * inv2
        dip = q[1] * u[0] + q[2] * u[1] + q[3] * u[2]
        quad = [q[4 + 3 * a] * u[0] + q[5 + 3 * a] * u[1] + q[6 + 3 * a] * u[2] for a in range(3)]
        form = quad[0] * u[0] + quad[1] * u[1] + quad[2] * u[2]
        trace = q[4] + q[8] + q[12]
        radial = (1.5 * trace - 3.0 * dip) * inv5 - q[0] * inv3 - 7.5 * form * inv7
        return tuple(grads[c] + u[c] * radial + q[1 + c] * inv3 + 3.0 * quad[c] * inv5
                     for c in range(3))

    zero = jnp.zeros((8, width), F32)
    grads = lax.fori_loop(0, kcount, far_step, (zero, zero, zero))
    for c in range(3):
        far[c] = grads[c]
    for rep in [(a, b, r) for r in [0] + zs for a in [0] + xs for b in [0] + ys]:
        if rep != (0, 0, 0):
            arrived(rep)

    for step in range(1, 8):
        part_copy(step).wait_send()
    for copy in copies.values():
        copy.wait_send()
    for slot in range(blocks.shape[0]):
        ctrl[slot] = blocks[slot, :, 9 * seg:9 * seg + 128]


def force_kernel(dims, scalars, blocks, held, own, far, out,
                 feat, wide, tall, rows, cols, high0, low0, high1, low1, acc, todo):
    me = tuple(lax.axis_index(a) for a in AXES)
    tiles = held.shape[0] - 1
    seg = tiles * LANES
    width = seg // 8
    for buf in (feat, wide, tall, high1, low1):
        buf[...] = jnp.zeros_like(buf)
    acc[...] = own[...]
    def list_source(t, carry):
        at, found = carry
        slot = slot_index(dims, (t // 9 - 1, t // 3 % 3 - 1, t % 3 - 1))
        ahead = t > 13
        flag = scalars[jnp.where(ahead, 0, slot), 0,
                       jnp.where(ahead, t - 14, jnp.maximum(12 - t, 0))]
        listed = jnp.logical_and(t != 13, flag > 0.0)
        todo[0, found] = t
        todo[1, found] = at
        size = (scalars[slot, 0, 13].astype(jnp.int32) + (GRAIN - 1)) // GRAIN * GRAIN
        return at + jnp.where(listed, size, 0), found + listed.astype(jnp.int32)

    total, found = lax.fori_loop(0, 27, list_source, (0, 0))
    for k in range(2):
        todo[0, found + k] = 13
        todo[1, found + k] = total

    def three_sources(i, carry):
        laid = []
        for k in range(3):
            t, at = todo[0, 3 * i + k], todo[1, 3 * i + k]
            offset = (t // 9 - 1, t // 3 % 3 - 1, t % 3 - 1)
            slot = slot_index(dims, offset)

            def row(c, slot=slot):
                return blocks[slot, :, c * seg:(c + 1) * seg]

            y = [row(c) + (offset[c].astype(F32) - 0.5) for c in range(3)]
            laid.append((at, lay_sources(row, y, feat.at[k], wide.at[k], tall.at[k])))
        for at, (row_part, col_part) in laid:
            here = pl.ds(pl.multiple_of(at, GRAIN), seg)
            rows[here, :] = row_part
            cols[:, here] = col_part
        return carry

    lax.fori_loop(0, (found + 2) // 3, three_sources, 0)
    lane = lax.broadcasted_iota(jnp.int32, (ROWS, 128), 1)
    rows[pl.ds(pl.multiple_of(total, GRAIN), ROWS), :] = (lane == 3).astype(F32).astype(BF16)
    cols[:, pl.ds(pl.multiple_of(total, GRAIN), ROWS)] = jnp.zeros((16, ROWS), BF16)

    my_tiles = (scalars[0, 0, 13].astype(jnp.int32) + (LANES - 1)) // LANES
    spans = (total + (ROWS - 1)) // ROWS
    steps = my_tiles * spans
    buffers = ((high0, low0), (high1, low1))

    def place(step):
        done = step >= steps
        tile = jnp.where(done, tiles, step // spans)
        return tile, jnp.where(done, 0, step % spans)

    def some_steps(first, many):
        for k in range(many):
            strengths(held, rows, *place(first + k), buffers[k % 2])
            gather_force(cols, acc, *place(jnp.maximum(first + k - 1, 0)), buffers[1 - k % 2])

    def many_steps(i, carry):
        some_steps(i * UNROLL, UNROLL)
        return carry

    def two_steps(i, carry):
        some_steps(i * 2, 2)
        return carry

    def four_steps(i, carry):
        some_steps(i * 4, 4)
        return carry

    groups = steps // UNROLL
    fours = steps // 4
    pairs = (steps + 1) // 2
    lax.fori_loop(0, groups, many_steps, 0)
    lax.fori_loop(groups * (UNROLL // 4), fours, four_steps, 0)
    lax.fori_loop(fours * 2, pairs, two_steps, 0)

    @pl.when(pairs > 0)
    def _():
        gather_force(cols, acc, *place(pairs * 2 - 1), buffers[1])


    slot_id = lax.broadcasted_iota(jnp.int32, (8, width), 0) * width + lax.broadcasted_iota(
        jnp.int32, (8, width), 1)
    alive = (slot_id.astype(F32) < scalars[0, 0, 13]).astype(F32)
    for c in range(3):
        for t in range(tiles):
            turned = acc[t]
            near = (blocks[0, :, c * seg + t * LANES:c * seg + (t + 1) * LANES] - 0.5) * turned[4:5] - (turned[c:c + 1] + turned[8 + c:9 + c] + turned[12 + c:13 + c])
            for s in range(t * LANES // width, (t + 1) * LANES // width):
                inside = slice(s * width - t * LANES, (s + 1) * width - t * LANES)
                out[c, :, s * width:(s + 1) * width] = (near[:, inside] - far[c, s:s + 1]) * alive[s:s + 1]


def on_device(dims, midpoints, line_vectors, burgers, live_mask, pair_list):
    seg = midpoints.shape[4]
    count = dims[0] * dims[1] * dims[2]
    kcount = count // 8
    slots = len(reps(dims[0])) * len(reps(dims[1])) * len(reps(dims[2]))
    vmem = pl.BlockSpec(memory_space=pltpu.VMEM)
    smem = pl.BlockSpec(memory_space=pltpu.SMEM)
    hbm = pl.BlockSpec(memory_space=pltpu.HBM)
    strength_buffer = pltpu.VMEM((PARTS, ROWS, 128), BF16)
    targets = (seg // LANES + 1, 2 * PARTS, 128, 128)
    sums = (seg // LANES + 1, 16, LANES)
    blocks, ctrl, held, own, far = pl.pallas_call(
        functools.partial(gather_kernel, dims),
        out_shape=(jax.ShapeDtypeStruct((slots, 1, 9 * seg + 128), F32),
                   jax.ShapeDtypeStruct((slots, 1, 128), F32),
                   jax.ShapeDtypeStruct(targets, BF16),
                   jax.ShapeDtypeStruct(sums, F32),
                   jax.ShapeDtypeStruct((3, 8, seg // 8), F32)),
        in_specs=[hbm] * 5,
        out_specs=(vmem,) * 5,
        scratch_shapes=[
            pltpu.VMEM((16, seg), F32),
            pltpu.VMEM((128, seg), F32),
            pltpu.VMEM((8, 1, 128), F32),
            pltpu.VMEM((kcount, 1, 128), F32),
            pltpu.SMEM((kcount, 1, 128), F32),
            pltpu.VMEM((9, 8, seg // 8), F32),
            pltpu.VMEM((1, seg), jnp.int32),
            pltpu.VMEM((1, 13), jnp.int32),
            pltpu.VMEM((8, seg), F32),
            pltpu.VMEM((128, seg), F32),
            pltpu.VMEM((seg, 128), BF16),
            pltpu.VMEM((16, seg), BF16),
            *[strength_buffer] * 4,
            pltpu.SemaphoreType.DMA((6,)),
            pltpu.SemaphoreType.DMA((slots,)),
            pltpu.SemaphoreType.DMA((slots,)),
            pltpu.SemaphoreType.DMA((8,)),
            pltpu.SemaphoreType.DMA((8,)),
            pltpu.SemaphoreType.DMA((kcount,)),
            pltpu.SemaphoreType.DMA((kcount,)),
        ],
        compiler_params=pltpu.CompilerParams(collective_id=0, has_side_effects=True),
        name="gather",
    )(*(a.reshape(1, 3 * seg) for a in (midpoints, line_vectors, burgers)),
      live_mask.reshape(1, seg), pair_list.reshape(1, 13))
    out = pl.pallas_call(
        functools.partial(force_kernel, dims),
        out_shape=jax.ShapeDtypeStruct((3, 1, seg), F32),
        in_specs=[smem] + [vmem] * 4,
        out_specs=vmem,
        scratch_shapes=[
            pltpu.VMEM((3, 8, seg), F32),
            pltpu.VMEM((3, 16, seg), F32),
            pltpu.VMEM((3, 128, seg), F32),
            pltpu.VMEM((27 * seg + ROWS, 128), BF16),
            pltpu.VMEM((16, 27 * seg + ROWS), BF16),
            *[strength_buffer] * 4,
            pltpu.VMEM(sums, F32),
            pltpu.SMEM((2, 32), jnp.int32),
        ],
        compiler_params=pltpu.CompilerParams(vmem_limit_bytes=60 * 2**20),
        name="forces",
    )(ctrl, blocks, held, own, far)
    return out.reshape(3, 1, 1, 1, seg)


def solution(mesh):
    dims = tuple(mesh.shape[a] for a in AXES)
    placed = (
        P(None, "gx", "gy", "gz", None),
        P(None, "gx", "gy", "gz", None),
        P(None, "gx", "gy", "gz", None),
        P("gx", "gy", "gz", None),
        P(None, "gx", "gy", "gz"),
    )
    return jax.shard_map(
        functools.partial(on_device, dims),
        mesh=mesh,
        in_specs=placed,
        out_specs=P(None, "gx", "gy", "gz", None),
        check_vma=False,
    )
```
